256 devices in a mesh: dp: 8 (over y, core), expert: 32 (over x, z).
Axes of the slice: x: 4, y: 4, z: 8, core: 2. Of those that a mesh axis runs over, the one named last changes fastest.
Arguments:
- tokens: bfloat16 [32768, 1536], P(('dp', 'expert')), may hold values from -24 to 24
- out_grad: bfloat16 [32768, 1536], P(('dp', 'expert')), may hold values from -24 to 24
- logits: float32 [32768, 16], P(('dp', 'expert')), may hold values from -8 to 8
- routes: int32 [32768, 16], P(('dp', 'expert')), may hold values from 0 to 255, all different within a row; in each aligned block of 128 rows (0 to 127, 128 to 255, ...) at most 9 rows name the same one
- w_up: bfloat16 [256, 1536, 128], P('expert'), may hold values from -0.15625 to 0.15625
- w_down: bfloat16 [256, 1536, 128], P('expert'), may hold values from -0.15625 to 0.15625
Outputs:
- grad_tokens: bfloat16 [32768, 1536], P(('dp', 'expert'))
- grad_logits: float32 [32768, 16], P(('dp', 'expert'))
- grad_up: float32 [256, 1536, 128], P('expert', 'dp')
- grad_down: float32 [256, 1536, 128], P('expert', 'dp')
The draws below stay inside these ranges and needn't reach their ends.
Inputs may be any that keep to these rules, and one draw needn't show every extreme that they name: `routes`: each row names 16 different experts. Within the rows of one device no expert is named by more than 9 rows, and every draw has some device and expert with exactly 9.
All inputs are finite; a program needn't handle non-finite values.
Results may differ from the reference program's by a relative error of at most 0.012.
Values may be sent and summed in bfloat16 or wider, within the bound.
No kernel may reach another device: no remote copies, remote signals or barrier semaphores. Data moves between devices by JAX's collectives and lax.ppermute only.
A program may use at most 128 MiB of HBM per device.

```python
import math
import jax
import jax.numpy as jnp
import numpy as np
from jax import lax

D = 1536
H = 128
TOP = 16
TOK_DEV = 128
EXPERTS = 256
TOKENS = 32768
CAP = 9
N_DP = 8
N_EXPERT = 32


def raised(array, stream_key, source, target, blocks, factor):
    def block_of(axis_at):
        return (jnp.arange(array.shape[axis_at]) // (array.shape[axis_at] // blocks)).reshape((-1,) + (1,) * (array.ndim - 1 - axis_at))

    one_side = jax.random.permutation(stream_key, blocks)[block_of(target)]
    other_side = (block_of(target) + blocks // 2) % blocks
    return jnp.where((block_of(source) == one_side) | (block_of(source) == other_side), factor * array, array)


def block_levels(own_key, shape, split, least, top_value):
    def one(axis_at, blocks):
        heights = jax.random.uniform(jax.random.fold_in(jax.random.fold_in(own_key, 6), axis_at), (blocks,), jnp.float32, least / len(split), top_value / len(split))
        return jnp.repeat(jnp.exp(heights), shape[axis_at] // blocks).reshape((-1,) + (1,) * (len(shape) - axis_at - 1))

    level = one(*split[0])
    for cut in split[1:]:
        level = level * one(*cut)
    return level


def assign_block(own_key, own, number, rows, number_of, top, bound, skew):
    sequence = jax.random.permutation(own_key, number_of)
    packed, common = shares(number_of, rows * top, bound, skew, True), shares(number_of, rows * top, bound, skew, False)
    places = jnp.arange(number_of)

    def named(lengths, rotation):
        used = int((lengths > 0).sum())
        fixed = max(1, used // 4)
        moved = fixed + (places - fixed + rotation * (used - fixed)) % max(1, number_of - fixed)
        return jnp.zeros((number_of,), jnp.int32).at[sequence[jnp.where(places < fixed, places, moved)]].set(jnp.asarray(lengths, jnp.int32))

    lengths = jnp.where(number % 4 == 0, named(packed, number // 4), named(common, number - number // 4 - 1))
    mixed = jax.random.permutation(jax.random.fold_in(own, 3), number_of)
    giver, taker = mixed[0:number_of // 2 * 2:2], mixed[1:number_of // 2 * 2:2]
    room = jnp.minimum(lengths[giver] - 1, bound - lengths[taker]) // 2
    room = jnp.where((giver == sequence[0]) | (taker == sequence[0]) | (lengths[taker] == 0), 0, jnp.maximum(room, 0))
    moved = jax.random.randint(jax.random.fold_in(own, 4), (number_of // 2,), 0, 1 << 20) % (room + 1)
    lengths = lengths.at[giver].add(-moved).at[taker].add(moved)
    labels = jnp.searchsorted(jnp.cumsum(lengths), jnp.arange(rows * top), side="right").astype(jnp.int32)
    listing = labels.reshape(top, rows).T
    listing = listing[jax.random.permutation(jax.random.fold_in(own, 1), rows)]
    rotation = jax.random.randint(jax.random.fold_in(own, 2), (rows, 1), 0, top)
    return jnp.take_along_axis(listing, (jnp.arange(top)[None, :] + rotation) % top, axis=1)


def shares(amount, total, reach, skew, full):
    loads = [(1 << 20) // math.isqrt(rank ** skew) + 1 for rank in range(1, amount + 1)]
    largest = reach if full else min(reach, max(-(-total // amount), total * loads[0] // sum(loads)))
    least = 1 if total - largest >= amount - 1 else 0
    holding, rest = [largest] + [least] * (amount - 1), total - largest - least * (amount - 1)
    while rest > 0:
        movable = [i for i in range(1, amount) if holding[i] < largest] or [i for i in range(1, amount) if holding[i] < reach]
        whole, budget = sum([loads[i] for i in movable]), rest
        for i in movable:
            more = min(reach - holding[i], max(1, budget * loads[i] // whole), rest)
            holding[i] = holding[i] + more
            rest = rest - more
    return np.array(holding)


def centred(key, shape, scale, reach, pieces=(), kind=jnp.bfloat16):
    level = block_levels(key, shape, pieces, -0.22, 0.18) if pieces else 1.0
    array = jax.random.normal(key, shape, jnp.float32) * scale * level
    return jnp.minimum(jnp.maximum(array, -reach), reach).astype(kind)


def noise_with(key, dims, width, reach, cuts, heavy, kind=jnp.bfloat16):
    drawn = width * jax.random.normal(key, dims, jnp.float32)
    if cuts:
        drawn = drawn * block_levels(key, dims, cuts, -0.22, 0.18)
    return jnp.clip(raised(drawn, jax.random.fold_in(key, 3), *heavy), -reach, reach).astype(kind)


def setup_inputs(seed: int = 0) -> dict:
    key_list = jax.random.split(jax.random.key(seed), 7)
    tokens = noise_with(key_list[0], (TOKENS, D), 1.0, 24.0, ((0, 256),), (0, 1, 256, 6.0))
    out_grad = noise_with(key_list[1], (TOKENS, D), 1.0, 24.0, ((0, 256),), (0, 1, 256, 6.0))
    logits = centred(key_list[2], (TOKENS, TOP), 2.0, 8.0, ((0, 256),), jnp.float32)
    routes_keys = jax.random.split(jax.random.fold_in(key_list[3], 1), TOKENS // TOK_DEV)
    routes_turns = jax.random.permutation(jax.random.fold_in(key_list[3], 3), TOKENS // TOK_DEV)
    routes = jax.vmap(lambda own, number: assign_block(jax.random.fold_in(key_list[3], 2), own, number, TOK_DEV, EXPERTS, TOP, CAP, 1))(routes_keys, routes_turns).reshape((TOKENS, TOP))
    w_up = centred(key_list[4], (EXPERTS, D, H), D ** -0.5, 0.15625, ((0, 32),))
    w_down = centred(key_list[5], (EXPERTS, D, H), D ** -0.5, 0.15625, ((0, 32),))
    return dict(tokens=tokens, out_grad=out_grad, logits=logits, routes=routes, w_up=w_up, w_down=w_down)


gelu_scale = 0.7978845608028654
gelu_cubic = 0.044715


def gelu_pair(pre_act):
    inner_arg = gelu_scale * (pre_act + gelu_cubic * pre_act * pre_act * pre_act)
    tanh_val = jnp.tanh(inner_arg)
    act_value = 0.5 * pre_act * (1.0 + tanh_val)
    act_slope = 0.5 * (1.0 + tanh_val) + 0.5 * pre_act * (1.0 - tanh_val * tanh_val) * gelu_scale * (1.0 + 3.0 * gelu_cubic * pre_act * pre_act)
    return act_value, act_slope


def reference(tokens, out_grad, logits, routes, w_up, w_down):
    group_rows = TOK_DEV * N_EXPERT
    rows_max = CAP * N_EXPERT
    scores = jax.nn.sigmoid(logits)
    flat_scores = scores.reshape(-1)

    def per_expert(state_pair, expert_in):
        expert, up_mat, down_mat = expert_in

        def per_group(inner_state, group_idx):
            grad_rows, inner_acc = inner_state
            start = (group_idx * group_rows).astype(jnp.int32)
            block_ids = lax.dynamic_slice_in_dim(routes, start, group_rows, 0).reshape(-1)
            matches = block_ids == expert
            found_idx = jnp.nonzero(matches, size=rows_max, fill_value=0)[0].astype(jnp.int32)
            is_live = jnp.arange(rows_max, dtype=jnp.int32) < jnp.sum(matches.astype(jnp.int32))
            flat_idx = (start * TOP + found_idx).astype(jnp.int32)
            token_idx = (flat_idx // TOP).astype(jnp.int32)
            in_rows = jnp.where(is_live[:, None], tokens[token_idx], jnp.zeros((), jnp.bfloat16))
            gate_val = jnp.where(is_live, flat_scores[flat_idx], jnp.zeros((), jnp.float32))
            scaled_grad = (gate_val[:, None] * out_grad[token_idx].astype(jnp.float32)).astype(jnp.bfloat16)
            pre_act = jnp.dot(in_rows, up_mat, preferred_element_type=jnp.float32)
            act_value, act_slope = gelu_pair(pre_act)
            hidden = act_value.astype(jnp.bfloat16)
            grad_hidden = jnp.dot(scaled_grad, down_mat, preferred_element_type=jnp.float32)
            inner_prod = lax.optimization_barrier(jnp.sum(hidden.astype(jnp.float32) * grad_hidden, axis=1).astype(jnp.bfloat16))
            grad_pre = (grad_hidden * act_slope).astype(jnp.bfloat16)
            row_grads = jnp.dot(grad_pre, up_mat.T, preferred_element_type=jnp.float32).astype(jnp.bfloat16)
            up_grad = lax.optimization_barrier(jnp.dot(in_rows.T, grad_pre, preferred_element_type=jnp.float32).astype(jnp.bfloat16))
            down_grad = lax.optimization_barrier(jnp.dot(scaled_grad.T, hidden, preferred_element_type=jnp.float32).astype(jnp.bfloat16))
            grad_rows = grad_rows.at[token_idx].add(row_grads.astype(jnp.float32))
            inner_acc = inner_acc.at[flat_idx].add(inner_prod.astype(jnp.float32))
            return (grad_rows, inner_acc), (up_grad, down_grad)

        state_pair, parts = lax.scan(per_group, state_pair, jnp.arange(N_DP, dtype=jnp.int32))
        up_parts, down_parts = parts
        return state_pair, (jnp.sum(up_parts.astype(jnp.float32), axis=0), jnp.sum(down_parts.astype(jnp.float32), axis=0))

    init = (jnp.zeros((TOKENS, D), jnp.float32), jnp.zeros((TOKENS * TOP,), jnp.float32))
    final_state, grads = lax.scan(per_expert, init, (jnp.arange(EXPERTS, dtype=jnp.int32), w_up, w_down))
    grad_rows, inner_acc = final_state
    grad_up, grad_down = grads
    grad_tokens = grad_rows.astype(jnp.bfloat16)
    grad_logits = (1.0 - scores) * inner_acc.reshape(TOKENS, TOP)
    return grad_tokens, grad_logits, grad_up, grad_down
```

```python
import jax
import jax.numpy as jnp
from jax import lax
from jax.sharding import PartitionSpec as P

NX, NZ = 4, 8
CAP = 16
gelu_scale = 0.7978845608028654
gelu_cubic = 0.044715
bf16, f32 = jnp.bfloat16, jnp.float32


def gelu_pair(pre_act):
    inner_arg = gelu_scale * (pre_act + gelu_cubic * pre_act * pre_act * pre_act)
    tanh_val = jnp.tanh(inner_arg)
    act_value = 0.5 * pre_act * (1.0 + tanh_val)
    act_slope = 0.5 * (1.0 + tanh_val) + 0.5 * pre_act * (
        1.0 - tanh_val * tanh_val
    ) * gelu_scale * (1.0 + 3.0 * gelu_cubic * pre_act * pre_act)
    return (act_value, act_slope)


def ring(dx, dz):
    return [
        (x * NZ + z, ((x + dx) % NX) * NZ + (z + dz) % NZ) for x in range(NX) for z in range(NZ)
    ]


XP, XM, ZP, ZM = ring(1, 0), ring(-1, 0), ring(0, 1), ring(0, -1)
ZGROUPS = [[x * NZ + z for z in range(NZ)] for x in range(NX)]


def pp(value, perm):
    return lax.ppermute(value, "expert", perm)


def zgather(value):
    return lax.all_gather(value, "expert", axis_index_groups=ZGROUPS, tiled=False)


def add(*terms):
    total = terms[0].astype(f32)
    for term in terms[1:]:
        total = total + term.astype(f32)
    return total.astype(bf16)


def pick(array, index):
    return lax.dynamic_index_in_dim(array, index, 0, keepdims=False)


def reduce_x(blocks):
    half = blocks[2].shape[0] // 2
    via_m, via_p = pp(blocks[2][:half], XM), pp(blocks[2][half:], XP)
    low = jnp.concatenate([add(blocks[1][:half], via_m), blocks[1][half:]], 0)
    high = jnp.concatenate([blocks[3][:half], add(blocks[3][half:], via_p)], 0)
    from_p, from_m = pp(low, XM), pp(high, XP)
    return add(blocks[0], from_p, from_m)


def reduce_z(blocks, zi, split):
    at = lambda d: pick(blocks, (zi + d) % NZ)
    far = at(4)
    up, down = split(far)
    up, down = pp(up[0], ZP), pp(down[0], ZM)
    third_up, third_down = at(3), at(-3)
    a, b = split(third_up)
    up_sum = jnp.concatenate([add(a[0], up), a[1]], a[2])
    a, b = split(third_down)
    down_sum = jnp.concatenate([b[1], add(b[0], down)], b[2])
    up, down = pp(up_sum, ZP), pp(down_sum, ZM)
    for d in (2, 1):
        up, down = pp(add(at(d), up), ZP), pp(add(at(-d), down), ZM)
    return add(at(0), up, down)


def split_rows(axis):
    def split(value):
        half = value.shape[axis] // 2
        first = lax.slice_in_dim(value, 0, half, axis=axis)
        second = lax.slice_in_dim(value, half, None, axis=axis)
        return (first, second, axis), (second, first, axis)

    return split


def local(tokens, out_grad, logits, routes, w_up, w_down):
    tok, chosen = routes.shape
    exp_dev = w_up.shape[0]
    width, hid = w_up.shape[1], w_up.shape[2]
    experts = exp_dev * NX * NZ
    slots = exp_dev * CAP
    me = lax.axis_index("expert")
    xi, zi = me // NZ, me % NZ
    scores = jax.nn.sigmoid(logits)
    hit = routes[:, :, None] == jnp.arange(experts, dtype=jnp.int32)
    named = jnp.any(hit, axis=1).astype(bf16)
    before = jnp.tril(jnp.ones((tok, tok), bf16), -1)
    count = jnp.dot(before, named, preferred_element_type=f32)
    rank = jnp.sum(jnp.where(hit, count[:, None, :], 0.0), axis=2)
    info = jnp.concatenate([routes.astype(f32) * CAP + rank, scores], axis=1)
    infos = lax.all_gather(info, "expert").reshape(NX, NZ, tok, 2 * chosen)
    groups = 2 * width // 128
    cut = (7 * groups // 12) * 128
    pay = jnp.concatenate([tokens, out_grad], axis=1)
    pa, pb = pay[:, :cut], pay[:, cut:]
    az = zgather(pa)
    bp, bm = pp(pb, XP), pp(pb, XM)
    half = tok // 2
    b2 = jnp.concatenate([pp(bp[:half], XP), pp(bm[half:], XM)], 0)
    bz = zgather(jnp.stack([pb, bp, b2, bm]))
    ap, am = pp(az, XP), pp(az, XM)
    a2 = jnp.concatenate([pp(ap[: NZ // 2], XP), pp(am[NZ // 2 :], XM)], 0)
    parts = []
    for dx, a in enumerate((az, ap, a2, am)):
        inf = pick(infos, (xi - dx) % NX)
        slot = inf[:, :, :chosen] - (me * slots).astype(f32)
        gate = inf[:, :, chosen:]
        eq = slot[..., None] == jnp.arange(slots, dtype=jnp.int32).astype(f32)
        sel = jnp.any(eq, axis=2).astype(bf16)
        gate_slot = jnp.sum(jnp.where(eq, gate[..., None], 0.0), axis=(1, 2))
        xg = jnp.concatenate([a, bz[:, dx]], axis=2)
        picked = jnp.einsum("bts,btd->bsd", sel, xg, preferred_element_type=f32).astype(bf16)
        rows_x = picked[..., :width]
        rows_g = (gate_slot[..., None] * picked[..., width:].astype(f32)).astype(bf16)
        shape = (NZ, exp_dev, CAP, width)
        parts.append((eq, sel, rows_x.reshape(shape), rows_g.reshape(shape)))
    in_rows = jnp.concatenate([p[2] for p in parts], 0)
    in_grads = jnp.concatenate([p[3] for p in parts], 0)
    pre = jnp.einsum("becd,edh->bech", in_rows, w_up, preferred_element_type=f32)
    act_value, act_slope = gelu_pair(pre)
    hidden = act_value.astype(bf16)
    grad_hidden = jnp.einsum("becd,edh->bech", in_grads, w_down, preferred_element_type=f32)
    inner = jnp.sum(hidden.astype(f32) * grad_hidden, axis=-1).astype(bf16)
    grad_pre = (grad_hidden * act_slope).astype(bf16)
    row_grads = jnp.einsum("bech,edh->becd", grad_pre, w_up, preferred_element_type=f32).astype(
        bf16
    )
    up_grad = jnp.einsum("becd,bech->edh", in_rows, grad_pre, preferred_element_type=f32)
    down_grad = jnp.einsum("becd,bech->edh", in_grads, hidden, preferred_element_type=f32)
    back = []
    for dx in range(NX):
        eq, sel = parts[dx][0], parts[dx][1]
        rows = row_grads[dx * NZ : (dx + 1) * NZ].reshape(NZ, slots, width)
        summed = jnp.einsum("bts,bsd->btd", sel, rows, preferred_element_type=f32).astype(bf16)
        inn = inner[dx * NZ : (dx + 1) * NZ].reshape(NZ, 1, 1, slots).astype(f32)
        inn = jnp.sum(jnp.where(eq, inn, 0.0), axis=3).astype(bf16)
        inn = jnp.pad(inn, ((0, 0), (0, 0), (0, 128 - chosen)))
        back.append(jnp.concatenate([summed, inn], axis=2))
    total = width + 128
    cut = (7 * (total // 128) // 13) * 128
    in_a = [r[..., :cut] for r in back]
    in_b = jnp.stack([r[..., cut:] for r in back], axis=1)
    done_a = reduce_z(reduce_x(in_a), zi, split_rows(0))
    col_b = reduce_z(in_b, zi, split_rows(0))
    quarter = [col_b[dx] for dx in range(NX)]
    done_b = reduce_x(quarter)
    done = jnp.concatenate([done_a, done_b], axis=1)
    grad_tokens = done[:, :width]
    grad_logits = (1.0 - scores) * done[:, width : width + chosen].astype(f32)
    grad_up, grad_down = (
        lax.psum_scatter(g.astype(bf16), "dp", scatter_dimension=1, tiled=True).astype(f32)
        for g in (up_grad, down_grad)
    )
    return (grad_tokens, grad_logits, grad_up, grad_down)


def solution(mesh):
    rows = P(("dp", "expert"), None)
    weights = P("expert", None, None)
    grads = P("expert", "dp", None)
    return jax.shard_map(
        local,
        mesh=mesh,
        in_specs=(rows, rows, rows, rows, weights, weights),
        out_specs=(rows, rows, grads, grads),
        check_vma=False,
    )
```

```python
import jax
import jax.numpy as jnp
from jax import lax
from jax.experimental import pallas as pl
from jax.experimental.pallas import tpu as pltpu
from jax.sharding import PartitionSpec as P


NX, NZ = 4, 8
CAP = 16
gelu_scale = 0.7978845608028654
gelu_cubic = 0.044715
bf16, f32 = jnp.bfloat16, jnp.float32


def gelu_pair(pre_act):
    inner_arg = gelu_scale * (pre_act + gelu_cubic * pre_act * pre_act * pre_act)
    tanh_val = jnp.tanh(inner_arg)
    act_value = 0.5 * pre_act * (1.0 + tanh_val)
    act_slope = 0.5 * (1.0 + tanh_val) + 0.5 * pre_act * (
        1.0 - tanh_val * tanh_val
    ) * gelu_scale * (1.0 + 3.0 * gelu_cubic * pre_act * pre_act)
    return (act_value, act_slope)


GROUPS = ((0, 1, 7, 2), (6, 3, 5, 4))


def ring(dx, dz):
    return [
        (x * NZ + z, ((x + dx) % NX) * NZ + (z + dz) % NZ) for x in range(NX) for z in range(NZ)
    ]


XP, XM, ZP, ZM = ring(1, 0), ring(-1, 0), ring(0, 1), ring(0, -1)
ZGROUPS = [[x * NZ + z for z in range(NZ)] for x in range(NX)]
XGROUPS = [[x * NZ + z for x in range(NX)] for z in range(NZ)]


def pp(value, perm):
    return lax.ppermute(value, "expert", perm)


def zgather(value):
    return lax.all_gather(value, "expert", axis_index_groups=ZGROUPS, tiled=False)


def add(*terms):
    total = terms[0].astype(f32)
    for term in terms[1:]:
        total = total + term.astype(f32)
    return total.astype(bf16)


def expert_kernel(
    pos, info, *refs
):
    parts, refs = refs[: NX * len(GROUPS)], refs[NX * len(GROUPS) :]
    (b, w_up, w_down, oa, ob, xc_out, sc_out, gp_out, hid_out,
     abuf, bbuf, xc, sc, rc, ko, pt, stage, in_sem, out_sem, save_sem) = refs
    exp_dev, width, _ = w_up.shape
    slots = exp_dev * CAP
    tok = parts[0].shape[1]
    cut_in, cut_out = parts[0].shape[2], oa.shape[3]
    chosen = info.shape[2] // 2
    zi, xi = pos[0], pos[2]
    base = (pos[1] * slots).astype(f32)

    def turn(i):
        return jnp.where(lax.rem(i, 2) == 1, (i + 1) // 2, lax.rem(NZ - i // 2, NZ))

    def x_of(dx):
        return lax.rem(xi - dx + NX, NX)

    def source(i):
        return lax.rem(zi - turn(i) + NZ, NZ)

    def fetch_a(g, j, slot):
        own, plus, minus, far = parts[NX * g : NX * (g + 1)]
        return [
            pltpu.make_async_copy(part.at[j], abuf.at[slot, dx], in_sem.at[slot, dx])
            for dx, part in enumerate((own, plus, far, minus))
        ]

    def fetch_b(i, slot):
        return pltpu.make_async_copy(b.at[source(i)], bbuf.at[slot], in_sem.at[slot, NX])

    def begin(i, slot):
        fetch_b(i, slot).start()
        step = 0
        for g, turns in enumerate(GROUPS):
            for j in range(len(turns)):

                @pl.when(i == step)
                def _():
                    for copy in fetch_a(g, j, slot):
                        copy.start()

                step += 1

    begin(jnp.int32(0), 0)
    row = lax.broadcasted_iota(jnp.int32, (slots, tok), 0).astype(f32)
    lane = lax.broadcasted_iota(jnp.int32, (slots, 128), 1).astype(f32) + 1.0

    def select(z, carry):
        slot = lax.rem(z, 2)

        @pl.when(z + 1 < NZ)
        def _():
            begin(z + 1, 1 - slot)

        fetch_b(z, slot).wait()
        for copy in fetch_a(0, 0, slot):
            copy.wait()
        dz = source(z)
        rest = cut_in - width

        def block(dx, inner_carry):
            table = info.at[dz, x_of(dx)]
            which = jnp.zeros((slots, tok), f32)
            gates = jnp.zeros((slots, tok), f32)
            for k in range(chosen):
                eq = (table[k : k + 1, :] - base) == row
                which = jnp.where(eq, k + 1.0, which)
                gates = jnp.where(eq, table[chosen + k : chosen + k + 1, :], gates)
            sel = (which > 0.0).astype(f32)
            pt[z, dx] = sel.T.astype(bf16)
            sel = sel.astype(bf16)
            gate = jnp.sum(gates, axis=1, keepdims=True)
            span = pl.ds(pl.multiple_of(dx * CAP, CAP), CAP)
            ko[:, z, span, :] = (
                (jnp.sum(which, axis=1, keepdims=True) == lane)
                .astype(bf16)
                .reshape(exp_dev, CAP, 128)
            )
            rows = jnp.dot(sel, abuf[slot, dx, :, :width], preferred_element_type=f32)
            xc[:, z, span, :] = rows.astype(bf16).reshape(exp_dev, CAP, width)
            first = jnp.dot(sel, abuf[slot, dx, :, width:], preferred_element_type=f32)
            sc[:, z, span, :rest] = (gate * first).astype(bf16).reshape(exp_dev, CAP, rest)
            second = jnp.dot(sel, bbuf[slot, x_of(dx)], preferred_element_type=f32)
            sc[:, z, span, rest:] = (
                (gate * second).astype(bf16).reshape(exp_dev, CAP, width - rest)
            )
            return inner_carry

        lax.fori_loop(0, NX, block, 0)
        return carry

    lax.fori_loop(0, NZ, select, 0)

    def saves(e):
        return (
            pltpu.make_async_copy(xc.at[e], xc_out.at[e], save_sem.at[0, e]),
            pltpu.make_async_copy(sc.at[e], sc_out.at[e], save_sem.at[1, e]),
        )

    rows = NZ * NX * CAP

    def expert(e, carry):
        for copy in saves(e):
            copy.start()
        up = w_up[e]
        pre = jnp.dot(xc[e].reshape(rows, width), up, preferred_element_type=f32)
        act_value, act_slope = gelu_pair(pre)
        hidden = act_value.astype(bf16)
        grad_hidden = jnp.dot(
            sc[e].reshape(rows, width), w_down[e], preferred_element_type=f32
        )
        inner = jnp.sum(hidden.astype(f32) * grad_hidden, axis=1, keepdims=True)
        grad_pre = (grad_hidden * act_slope).astype(bf16)
        gp_out[e] = grad_pre
        hid_out[e] = hidden
        back = lax.dot_general(
            grad_pre, up, (((1,), (1,)), ((), ())), preferred_element_type=f32
        )
        rc[e, :, :, :width] = back.astype(bf16).reshape(NZ, NX * CAP, width)
        marks = ko[e].reshape(rows, 128).astype(f32) * inner
        rc[e, :, :, width:] = marks.astype(bf16).reshape(NZ, NX * CAP, 128)
        return carry

    lax.fori_loop(0, exp_dev, expert, 0)

    def flush(d, slot):
        copies = []
        for dx in range(NX):
            copies.append(
                pltpu.make_async_copy(
                    stage.at[slot, dx, :, pl.ds(0, cut_out)],
                    oa.at[x_of(dx), d],
                    out_sem.at[slot, dx],
                )
            )
            copies.append(
                pltpu.make_async_copy(
                    stage.at[slot, dx, :, pl.ds(cut_out, width + 128 - cut_out)],
                    ob.at[lax.rem(d - zi + NZ, NZ), dx],
                    out_sem.at[slot, NX + dx],
                )
            )
        return copies

    def drain(slot):
        for copy in flush(0, slot):
            copy.wait()

    def combine(step, carry):
        slot = lax.rem(step, 2)
        d = source(step)

        @pl.when(step >= 2)
        def _():
            drain(slot)

        for dx in range(NX):
            picked = rc[:, step, dx * CAP : (dx + 1) * CAP, :].reshape(slots, width + 128)
            total = jnp.dot(pt[step, dx], picked, preferred_element_type=f32)
            stage[slot, dx] = total.astype(bf16)
        for copy in flush(d, slot):
            copy.start()
        return carry

    lax.fori_loop(0, NZ, combine, 0)
    drain(0)
    drain(1)

    def finish(e, carry):
        for copy in saves(e):
            copy.wait()
        return carry

    lax.fori_loop(0, exp_dev, finish, 0)


def expert_call(pos, info, parts, b, w_up, w_down, cut_out):
    exp_dev, width, hid = w_up.shape
    tok, cut_in = parts[0].shape[1], parts[0].shape[2]
    slots, rows = exp_dev * CAP, NZ * NX * CAP
    wide = width + 128
    shape = jax.ShapeDtypeStruct
    vmem = pl.BlockSpec(memory_space=pltpu.VMEM)
    hbm = pl.BlockSpec(memory_space=pl.ANY)
    flops = 2 * exp_dev * rows * width * hid * 3 + 2 * NZ * NX * slots * tok * width * 3
    return pl.pallas_call(
        expert_kernel,
        out_shape=(
            shape((NX, NZ, tok, cut_out), bf16),
            shape((NZ, NX, tok, wide - cut_out), bf16),
            shape((exp_dev, NZ, NX * CAP, width), bf16),
            shape((exp_dev, NZ, NX * CAP, width), bf16),
            shape((exp_dev, rows, hid), bf16),
            shape((exp_dev, rows, hid), bf16),
        ),
        in_specs=[pl.BlockSpec(memory_space=pltpu.SMEM), vmem] + [hbm] * (NX * len(GROUPS) + 1) + [vmem] * 2,
        out_specs=tuple([hbm] * 4 + [vmem] * 2),
        scratch_shapes=[
            pltpu.VMEM((2, NX, tok, cut_in), bf16),
            pltpu.VMEM((2, NX, tok, 2 * width - cut_in), bf16),
            pltpu.VMEM((exp_dev, NZ, NX * CAP, width), bf16),
            pltpu.VMEM((exp_dev, NZ, NX * CAP, width), bf16),
            pltpu.VMEM((exp_dev, NZ, NX * CAP, wide), bf16),
            pltpu.VMEM((exp_dev, NZ, NX * CAP, 128), bf16),
            pltpu.VMEM((NZ, NX, tok, slots), bf16),
            pltpu.VMEM((2, NX, tok, wide), bf16),
            pltpu.SemaphoreType.DMA((2, NX + 1)),
            pltpu.SemaphoreType.DMA((2, 2 * NX)),
            pltpu.SemaphoreType.DMA((2, exp_dev)),
        ],
        compiler_params=pltpu.CompilerParams(vmem_limit_bytes=62 * 1024 * 1024),
        cost_estimate=pl.CostEstimate(
            flops=flops, bytes_accessed=70 * 1024 * 1024, transcendentals=exp_dev * rows * hid
        ),
        name="experts",
    )(pos, info, *parts, b, w_up, w_down)


def exchange(value, groups):
    return lax.all_to_all(
        value, "expert", split_axis=0, concat_axis=0, axis_index_groups=groups, tiled=True
    )


def copies(value, n):
    return jnp.broadcast_to(value, (n, *value.shape))


def reduce_z(blocks):
    half = blocks.shape[1] // 2
    up, down = pp(blocks[4, :half], ZP), pp(blocks[4, half:], ZM)
    up, down = lax.optimization_barrier((up, down))
    up_sum = jnp.concatenate([add(blocks[3, :half], up), blocks[3, half:]], 0)
    down_sum = jnp.concatenate([blocks[5, :half], add(blocks[5, half:], down)], 0)
    up, down = pp(up_sum, ZP), pp(down_sum, ZM)
    for d in (2, 1):
        up, down = lax.optimization_barrier((up, down))
        up_sum, down_sum = add(blocks[d], up), add(blocks[NZ - d], down)
        up, down = pp(up_sum, ZP), pp(down_sum, ZM)
    return add(blocks[0], up, down)


def wgrad_kernel(rows, grads, out):
    flat = rows[0].reshape(grads.shape[1], rows.shape[3])
    total = lax.dot_general(
        flat, grads[0], (((0,), (0,)), ((), ())), preferred_element_type=f32
    )
    out[0] = total.astype(bf16)


def wgrad_call(rows, grads):
    exp_dev, width, hid = rows.shape[0], rows.shape[3], grads.shape[2]
    count = grads.shape[1]
    return pl.pallas_call(
        wgrad_kernel,
        grid=(exp_dev,),
        out_shape=jax.ShapeDtypeStruct((exp_dev, width, hid), bf16),
        in_specs=[
            pl.BlockSpec((1, *rows.shape[1:]), lambda e: (e, 0, 0, 0)),
            pl.BlockSpec((1, count, hid), lambda e: (e, 0, 0)),
        ],
        out_specs=pl.BlockSpec((1, width, hid), lambda e: (e, 0, 0)),
        compiler_params=pltpu.CompilerParams(vmem_limit_bytes=60 * 1024 * 1024),
        cost_estimate=pl.CostEstimate(
            flops=2 * exp_dev * count * width * hid,
            bytes_accessed=16 * 1024 * 1024,
            transcendentals=0,
        ),
        name="wgrad",
    )(rows, grads)


def final_kernel(za, own, b1, b2, b3, scores, tok_out, log_out):
    width, cut = tok_out.shape[1], za.shape[2]
    chosen = scores.shape[1]
    total = za[0].astype(f32)
    for z in range(1, NZ):
        total = total + za[z].astype(f32)
    tok_out[:, :cut] = total.astype(bf16)
    total = own[0].astype(f32)
    for other in (b1, b2, b3):
        total = total + other[...].astype(f32)
    tok_out[:, cut:] = total[:, : width - cut].astype(bf16)
    inner = total[:, width - cut : width - cut + chosen].astype(bf16).astype(f32)
    log_out[...] = (1.0 - scores[...]) * inner


def final_call(za, col, others, scores, width):
    tok = scores.shape[0]
    full = lambda v: pl.BlockSpec(v.shape, lambda i: (0,) * v.ndim)
    return pl.pallas_call(
        final_kernel,
        grid=(1,),
        out_shape=(
            jax.ShapeDtypeStruct((tok, width), bf16),
            jax.ShapeDtypeStruct(scores.shape, f32),
        ),
        in_specs=[full(za), pl.BlockSpec((1, *col.shape[1:]), lambda i: (0, 0, 0))]
        + [full(v) for v in others]
        + [full(scores)],
        out_specs=(
            pl.BlockSpec((tok, width), lambda i: (0, 0)),
            pl.BlockSpec(scores.shape, lambda i: (0, 0)),
        ),
        compiler_params=pltpu.CompilerParams(vmem_limit_bytes=24 * 1024 * 1024),
        name="final",
    )(za, col, *others, scores)


def gather_a(own):
    half = own.shape[0] // 2
    at = {0: own}
    up = down = own
    for d in range(1, 4):
        up, down = pp(up, ZP), pp(down, ZM)
        at[d], at[NZ - d] = up, down
    at[4] = jnp.concatenate([pp(up[:half], ZP), pp(down[half:], ZM)], 0)
    parts = []
    for g, turns in enumerate(GROUPS):
        group = jnp.stack([at[d] for d in turns])
        plus, minus = pp(group, XP), pp(group, XM)
        far = pp(minus, XM) if g else pp(plus, XP)
        parts += [group, plus, minus, far]
    return parts


def local(tokens, out_grad, logits, routes, w_up, w_down):
    tok, _ = routes.shape
    exp_dev, width, _ = w_up.shape
    experts = exp_dev * NX * NZ
    me = lax.axis_index("expert")
    scores = jax.nn.sigmoid(logits)
    hit = routes[:, :, None] == jnp.arange(experts, dtype=jnp.int32)
    named = jnp.any(hit, axis=1).astype(bf16)
    before = jnp.tril(jnp.ones((tok, tok), bf16), -1)
    count = jnp.dot(before, named, preferred_element_type=f32)
    rank = jnp.sum(jnp.where(hit, count[:, None, :], 0.0), axis=2)
    info = jnp.concatenate([routes.astype(f32) * CAP + rank, scores], axis=1).T
    groups = 2 * width // 128
    cut = (7 * groups // 12) * 128
    pay = jnp.concatenate([tokens, out_grad], axis=1)
    pa, pb = pay[:, :cut], pay[:, cut:]
    bx = exchange(copies(pb, NX), XGROUPS)
    bz = zgather(bx)
    column = exchange(copies(info, NX), XGROUPS)
    infos = exchange(copies(column, NZ), ZGROUPS)
    parts = gather_a(pa)
    wide = width + 128
    cut_out = (6 * (wide // 128) // 13) * 128
    pos = jnp.stack([me % NZ, me, me // NZ]).astype(jnp.int32)
    oa, ob, xc, sc, grad_pre, hidden = expert_call(
        pos, infos, parts, bz, w_up, w_down, cut_out
    )
    col_b = reduce_z(ob)
    ax = exchange(oa, XGROUPS)
    up_grad = wgrad_call(xc, grad_pre)
    down_grad = wgrad_call(sc, hidden)
    za = exchange(add(*[ax[x] for x in range(NX)]), ZGROUPS)
    others = [pp(col_b[dx], perm) for dx, perm in ((1, XM), (2, ring(2, 0)), (3, XP))]
    grad_tokens, grad_logits = final_call(za, col_b, others, scores, width)
    grad_up, grad_down = (
        lax.psum_scatter(g, "dp", scatter_dimension=1, tiled=True).astype(f32)
        for g in (up_grad, down_grad)
    )
    return (grad_tokens, grad_logits, grad_up, grad_down)


def solution(mesh):
    rows = P(("dp", "expert"), None)
    weights = P("expert", None, None)
    grads = P("expert", "dp", None)
    return jax.shard_map(
        local,
        mesh=mesh,
        in_specs=(rows, rows, rows, rows, weights, weights),
        out_specs=(rows, rows, grads, grads),
        check_vma=False,
    )
```

```python
import jax
import jax.numpy as jnp
from jax import lax
from jax.experimental import pallas as pl
from jax.experimental.pallas import tpu as pltpu
from jax.sharding import PartitionSpec as P


NX, NZ = 4, 8
CAP = 16
gelu_scale = 0.7978845608028654
gelu_cubic = 0.044715
bf16, f32 = jnp.bfloat16, jnp.float32


def gelu_pair(pre_act):
    inner_arg = gelu_scale * (pre_act + gelu_cubic * pre_act * pre_act * pre_act)
    tanh_val = jnp.tanh(inner_arg)
    act_value = 0.5 * pre_act * (1.0 + tanh_val)
    act_slope = 0.5 * (1.0 + tanh_val) + 0.5 * pre_act * (
        1.0 - tanh_val * tanh_val
    ) * gelu_scale * (1.0 + 3.0 * gelu_cubic * pre_act * pre_act)
    return (act_value, act_slope)


GROUPS = ((0, 1, 7, 2), (6, 3, 5, 4))


def ring(dx, dz):
    return [
        (x * NZ + z, ((x + dx) % NX) * NZ + (z + dz) % NZ) for x in range(NX) for z in range(NZ)
    ]


XP, XM, ZP, ZM = ring(1, 0), ring(-1, 0), ring(0, 1), ring(0, -1)
ZGROUPS = [[x * NZ + z for z in range(NZ)] for x in range(NX)]
XGROUPS = [[x * NZ + z for x in range(NX)] for z in range(NZ)]


def pp(value, perm):
    return lax.ppermute(value, "expert", perm)


def add(*terms):
    total = terms[0].astype(f32)
    for term in terms[1:]:
        total = total + term.astype(f32)
    return total.astype(bf16)


def expert_kernel(
    pos, info, *refs
):
    parts, refs = refs[: NX * len(GROUPS)], refs[NX * len(GROUPS) :]
    (b, w_up, w_down, oa, ob, xc_out, sc_out, gp_out, hid_out,
     abuf, bbuf, xc, sc, rc, ko, pt, stage, in_sem, out_sem, save_sem) = refs
    exp_dev, width, _ = w_up.shape
    slots = exp_dev * CAP
    tok = parts[0].shape[1]
    cut_in, cut_out = parts[0].shape[2], oa.shape[3]
    chosen = info.shape[2] // 2
    zi, xi = pos[0], pos[2]
    base = (pos[1] * slots).astype(f32)

    def turn(i):
        return jnp.where(lax.rem(i, 2) == 1, (i + 1) // 2, lax.rem(NZ - i // 2, NZ))

    def x_of(dx):
        return lax.rem(xi - dx + NX, NX)

    def source(i):
        return lax.rem(zi - turn(i) + NZ, NZ)

    def fetch_a(g, j, slot):
        own, plus, minus, far = parts[NX * g : NX * (g + 1)]
        return [
            pltpu.make_async_copy(part.at[j], abuf.at[slot, dx], in_sem.at[slot, dx])
            for dx, part in enumerate((own, plus, far, minus))
        ]

    def fetch_b(i, slot):
        return pltpu.make_async_copy(b.at[:, source(i)], bbuf.at[slot], in_sem.at[slot, NX])

    def begin(i, slot):
        fetch_b(i, slot).start()
        step = 0
        for g, turns in enumerate(GROUPS):
            for j in range(len(turns)):

                @pl.when(i == step)
                def _():
                    for copy in fetch_a(g, j, slot):
                        copy.start()

                step += 1

    begin(jnp.int32(0), 0)
    row = lax.broadcasted_iota(jnp.int32, (slots, tok), 0).astype(f32)
    lane = lax.broadcasted_iota(jnp.int32, (slots, 128), 1).astype(f32) + 1.0

    def select(z, carry):
        slot = lax.rem(z, 2)

        @pl.when(z + 1 < NZ)
        def _():
            begin(z + 1, 1 - slot)

        fetch_b(z, slot).wait()
        for copy in fetch_a(0, 0, slot):
            copy.wait()
        dz = source(z)
        rest = cut_in - width

        def block(dx, inner_carry):
            table = info.at[dz, x_of(dx)]
            which = jnp.zeros((slots, tok), f32)
            gates = jnp.zeros((slots, tok), f32)
            for k in range(chosen):
                eq = (table[k : k + 1, :] - base) == row
                which = jnp.where(eq, k + 1.0, which)
                gates = jnp.where(eq, table[chosen + k : chosen + k + 1, :], gates)
            sel = (which > 0.0).astype(f32)
            pt[z, dx] = sel.T.astype(bf16)
            sel = sel.astype(bf16)
            gate = jnp.sum(gates, axis=1, keepdims=True)
            span = pl.ds(pl.multiple_of(dx * CAP, CAP), CAP)
            ko[:, z, span, :] = (
                (jnp.sum(which, axis=1, keepdims=True) == lane)
                .astype(bf16)
                .reshape(exp_dev, CAP, 128)
            )
            rows = jnp.dot(sel, abuf[slot, dx, :, :width], preferred_element_type=f32)
            xc[:, z, span, :] = rows.astype(bf16).reshape(exp_dev, CAP, width)
            first = jnp.dot(sel, abuf[slot, dx, :, width:], preferred_element_type=f32)
            sc[:, z, span, :rest] = (gate * first).astype(bf16).reshape(exp_dev, CAP, rest)
            second = jnp.dot(sel, bbuf[slot, x_of(dx)], preferred_element_type=f32)
            sc[:, z, span, rest:] = (
                (gate * second).astype(bf16).reshape(exp_dev, CAP, width - rest)
            )
            return inner_carry

        lax.fori_loop(0, NX, block, 0)
        return carry

    lax.fori_loop(0, NZ, select, 0)

    def saves(e):
        return (
            pltpu.make_async_copy(xc.at[e], xc_out.at[e], save_sem.at[0, e]),
            pltpu.make_async_copy(sc.at[e], sc_out.at[e], save_sem.at[1, e]),
        )

    rows = NZ * NX * CAP

    def expert(e, carry):
        for copy in saves(e):
            copy.start()
        up = w_up[e]
        pre = jnp.dot(xc[e].reshape(rows, width), up, preferred_element_type=f32)
        act_value, act_slope = gelu_pair(pre)
        hidden = act_value.astype(bf16)
        grad_hidden = jnp.dot(
            sc[e].reshape(rows, width), w_down[e], preferred_element_type=f32
        )
        inner = jnp.sum(hidden.astype(f32) * grad_hidden, axis=1, keepdims=True)
        grad_pre = (grad_hidden * act_slope).astype(bf16)
        gp_out[e] = grad_pre
        hid_out[e] = hidden
        back = lax.dot_general(
            grad_pre, up, (((1,), (1,)), ((), ())), preferred_element_type=f32
        )
        rc[e, :, :, :width] = back.astype(bf16).reshape(NZ, NX * CAP, width)
        marks = ko[e].reshape(rows, 128).astype(f32) * inner
        rc[e, :, :, width:] = marks.astype(bf16).reshape(NZ, NX * CAP, 128)
        return carry

    lax.fori_loop(0, exp_dev, expert, 0)

    def flush(d, slot):
        copies = []
        for dx in range(NX):
            copies.append(
                pltpu.make_async_copy(
                    stage.at[slot, dx, :, pl.ds(0, cut_out)],
                    oa.at[x_of(dx), d],
                    out_sem.at[slot, dx],
                )
            )
            copies.append(
                pltpu.make_async_copy(
                    stage.at[slot, dx, :, pl.ds(cut_out, width + 128 - cut_out)],
                    ob.at[lax.rem(d - zi + NZ, NZ), dx],
                    out_sem.at[slot, NX + dx],
                )
            )
        return copies

    def drain(slot):
        for copy in flush(0, slot):
            copy.wait()

    def combine(step, carry):
        slot = lax.rem(step, 2)
        d = source(step)

        @pl.when(step >= 2)
        def _():
            drain(slot)

        for dx in range(NX):
            picked = rc[:, step, dx * CAP : (dx + 1) * CAP, :].reshape(slots, width + 128)
            total = jnp.dot(pt[step, dx], picked, preferred_element_type=f32)
            stage[slot, dx] = total.astype(bf16)
        for copy in flush(d, slot):
            copy.start()
        return carry

    lax.fori_loop(0, NZ, combine, 0)
    drain(0)
    drain(1)

    def finish(e, carry):
        for copy in saves(e):
            copy.wait()
        return carry

    lax.fori_loop(0, exp_dev, finish, 0)


def expert_call(pos, info, parts, b, w_up, w_down, cut_out):
    exp_dev, width, hid = w_up.shape
    tok, cut_in = parts[0].shape[1], parts[0].shape[2]
    slots, rows = exp_dev * CAP, NZ * NX * CAP
    wide = width + 128
    shape = jax.ShapeDtypeStruct
    vmem = pl.BlockSpec(memory_space=pltpu.VMEM)
    hbm = pl.BlockSpec(memory_space=pl.ANY)
    flops = 2 * exp_dev * rows * width * hid * 3 + 2 * NZ * NX * slots * tok * width * 3
    return pl.pallas_call(
        expert_kernel,
        out_shape=(
            shape((NX, NZ, tok, cut_out), bf16),
            shape((NZ, NX, tok, wide - cut_out), bf16),
            shape((exp_dev, NZ, NX * CAP, width), bf16),
            shape((exp_dev, NZ, NX * CAP, width), bf16),
            shape((exp_dev, rows, hid), bf16),
            shape((exp_dev, rows, hid), bf16),
        ),
        in_specs=[pl.BlockSpec(memory_space=pltpu.SMEM), vmem] + [hbm] * (NX * len(GROUPS) + 1) + [vmem] * 2,
        out_specs=tuple([hbm] * 4 + [vmem] * 2),
        scratch_shapes=[
            pltpu.VMEM((2, NX, tok, cut_in), bf16),
            pltpu.VMEM((2, NX, tok, 2 * width - cut_in), bf16),
            pltpu.VMEM((exp_dev, NZ, NX * CAP, width), bf16),
            pltpu.VMEM((exp_dev, NZ, NX * CAP, width), bf16),
            pltpu.VMEM((exp_dev, NZ, NX * CAP, wide), bf16),
            pltpu.VMEM((exp_dev, NZ, NX * CAP, 128), bf16),
            pltpu.VMEM((NZ, NX, tok, slots), bf16),
            pltpu.VMEM((2, NX, tok, wide), bf16),
            pltpu.SemaphoreType.DMA((2, NX + 1)),
            pltpu.SemaphoreType.DMA((2, 2 * NX)),
            pltpu.SemaphoreType.DMA((2, exp_dev)),
        ],
        compiler_params=pltpu.CompilerParams(vmem_limit_bytes=62 * 1024 * 1024),
        cost_estimate=pl.CostEstimate(
            flops=flops, bytes_accessed=70 * 1024 * 1024, transcendentals=exp_dev * rows * hid
        ),
        name="experts",
    )(pos, info, *parts, b, w_up, w_down)


def exchange(value, groups):
    return lax.all_to_all(
        value, "expert", split_axis=0, concat_axis=0, axis_index_groups=groups, tiled=True
    )


def copies(value, n):
    return jnp.broadcast_to(value, (n, *value.shape))


def reduce_z(blocks):
    half = blocks.shape[1] // 2
    up, down = pp(blocks[4, :half], ZP), pp(blocks[4, half:], ZM)
    up, down = lax.optimization_barrier((up, down))
    up_sum = jnp.concatenate([add(blocks[3, :half], up), blocks[3, half:]], 0)
    down_sum = jnp.concatenate([blocks[5, :half], add(blocks[5, half:], down)], 0)
    up, down = pp(up_sum, ZP), pp(down_sum, ZM)
    for d in (2, 1):
        up, down = lax.optimization_barrier((up, down))
        up_sum, down_sum = add(blocks[d], up), add(blocks[NZ - d], down)
        up, down = pp(up_sum, ZP), pp(down_sum, ZM)
    return add(blocks[0], up, down)


def wgrad_kernel(rows, grads, out):
    flat = rows[0].reshape(grads.shape[1], rows.shape[3])
    total = lax.dot_general(
        flat, grads[0], (((0,), (0,)), ((), ())), preferred_element_type=f32
    )
    out[0] = total.astype(bf16)


def wgrad_call(rows, grads):
    exp_dev, width, hid = rows.shape[0], rows.shape[3], grads.shape[2]
    count = grads.shape[1]
    return pl.pallas_call(
        wgrad_kernel,
        grid=(exp_dev,),
        out_shape=jax.ShapeDtypeStruct((exp_dev, width, hid), bf16),
        in_specs=[
            pl.BlockSpec((1, *rows.shape[1:]), lambda e: (e, 0, 0, 0)),
            pl.BlockSpec((1, count, hid), lambda e: (e, 0, 0)),
        ],
        out_specs=pl.BlockSpec((1, width, hid), lambda e: (e, 0, 0)),
        compiler_params=pltpu.CompilerParams(vmem_limit_bytes=60 * 1024 * 1024),
        cost_estimate=pl.CostEstimate(
            flops=2 * exp_dev * count * width * hid,
            bytes_accessed=16 * 1024 * 1024,
            transcendentals=0,
        ),
        name="wgrad",
    )(rows, grads)


def final_kernel(za, own, b1, b2, b3, scores, up, down, tok_out, log_out, up_out, down_out):
    width, cut = tok_out.shape[1], za.shape[2]
    chosen = scores.shape[1]
    total = za[0].astype(f32)
    for z in range(1, NZ):
        total = total + za[z].astype(f32)
    tok_out[:, :cut] = total.astype(bf16)
    total = own[0].astype(f32)
    for other in (b1, b2, b3):
        total = total + other[...].astype(f32)
    tok_out[:, cut:] = total[:, : width - cut].astype(bf16)
    inner = total[:, width - cut : width - cut + chosen].astype(bf16).astype(f32)
    log_out[...] = (1.0 - scores[...]) * inner
    up_out[...] = up[...].astype(f32)
    down_out[...] = down[...].astype(f32)


def final_call(za, col, others, scores, up, down, width):
    tok = scores.shape[0]
    full = lambda v: pl.BlockSpec(v.shape, lambda i: (0,) * v.ndim)
    return pl.pallas_call(
        final_kernel,
        grid=(1,),
        out_shape=(
            jax.ShapeDtypeStruct((tok, width), bf16),
            jax.ShapeDtypeStruct(scores.shape, f32),
            jax.ShapeDtypeStruct(up.shape, f32),
            jax.ShapeDtypeStruct(down.shape, f32),
        ),
        in_specs=[full(za), pl.BlockSpec((1, *col.shape[1:]), lambda i: (0, 0, 0))]
        + [full(v) for v in others]
        + [full(scores), full(up), full(down)],
        out_specs=(
            pl.BlockSpec((tok, width), lambda i: (0, 0)),
            full(scores),
            full(up),
            full(down),
        ),
        compiler_params=pltpu.CompilerParams(vmem_limit_bytes=24 * 1024 * 1024),
        name="final",
    )(za, col, *others, scores, up, down)


def gather_a(own):
    half = own.shape[0] // 2
    at = {0: own}
    up = down = own
    for d in range(1, 4):
        up, down = pp(up, ZP), pp(down, ZM)
        at[d], at[NZ - d] = up, down
    at[4] = jnp.concatenate([pp(up[:half], ZP), pp(down[half:], ZM)], 0)
    parts = []
    for g, turns in enumerate(GROUPS):
        group = jnp.stack([at[d] for d in turns])
        plus, minus = pp(group, XP), pp(group, XM)
        far = pp(minus, XM) if g else pp(plus, XP)
        parts += [group, plus, minus, far]
    return parts


def local(tokens, out_grad, logits, routes, w_up, w_down):
    tok, _ = routes.shape
    exp_dev, width, _ = w_up.shape
    experts = exp_dev * NX * NZ
    me = lax.axis_index("expert")
    scores = jax.nn.sigmoid(logits)
    hit = routes[:, :, None] == jnp.arange(experts, dtype=jnp.int32)
    named = jnp.any(hit, axis=1).astype(bf16)
    before = jnp.tril(jnp.ones((tok, tok), bf16), -1)
    count = jnp.dot(before, named, preferred_element_type=f32)
    rank = jnp.sum(jnp.where(hit, count[:, None, :], 0.0), axis=2)
    info = jnp.concatenate([routes.astype(f32) * CAP + rank, scores], axis=1).T
    groups = 2 * width // 128
    cut = (7 * groups // 12) * 128
    pay = jnp.concatenate([tokens, out_grad], axis=1)
    pa, pb = pay[:, :cut], pay[:, cut:]
    b_all = lax.all_gather(pb, "expert").reshape(NX, NZ, *pb.shape)
    column = exchange(copies(info, NX), XGROUPS)
    infos = exchange(copies(column, NZ), ZGROUPS)
    parts = gather_a(pa)
    wide = width + 128
    cut_out = (5 * (wide // 128) // 13) * 128
    pos = jnp.stack([me % NZ, me, me // NZ]).astype(jnp.int32)
    oa, ob, xc, sc, grad_pre, hidden = expert_call(
        pos, infos, parts, b_all, w_up, w_down, cut_out
    )
    col_b = reduce_z(ob)
    ax = exchange(oa, XGROUPS)
    up_grad = wgrad_call(xc, grad_pre)
    down_grad = wgrad_call(sc, hidden)
    za = exchange(add(*[ax[x] for x in range(NX)]), ZGROUPS)
    others = [pp(col_b[dx], perm) for dx, perm in ((1, XM), (2, ring(2, 0)), (3, XP))]
    up, down = (
        lax.psum_scatter(g, "dp", scatter_dimension=1, tiled=True) for g in (up_grad, down_grad)
    )
    return final_call(za, col_b, others, scores, up, down, width)


def solution(mesh):
    rows = P(("dp", "expert"), None)
    weights = P("expert", None, None)
    grads = P("expert", "dp", None)
    return jax.shard_map(
        local,
        mesh=mesh,
        in_specs=(rows, rows, rows, rows, weights, weights),
        out_specs=(rows, rows, grads, grads),
        check_vma=False,
    )
```

```python
import jax
import jax.numpy as jnp
from jax import lax
from jax.experimental import pallas as pl
from jax.experimental.pallas import tpu as pltpu
from jax.sharding import PartitionSpec as P


NX, NZ = 4, 8
CAP = 16
gelu_scale = 0.7978845608028654
gelu_cubic = 0.044715
bf16, f32 = jnp.bfloat16, jnp.float32


def gelu_pair(pre_act):
    inner_arg = gelu_scale * (pre_act + gelu_cubic * pre_act * pre_act * pre_act)
    tanh_val = jnp.tanh(inner_arg)
    act_value = 0.5 * pre_act * (1.0 + tanh_val)
    act_slope = 0.5 * (1.0 + tanh_val) + 0.5 * pre_act * (
        1.0 - tanh_val * tanh_val
    ) * gelu_scale * (1.0 + 3.0 * gelu_cubic * pre_act * pre_act)
    return (act_value, act_slope)


def ring(dx, dz):
    return [
        (x * NZ + z, ((x + dx) % NX) * NZ + (z + dz) % NZ) for x in range(NX) for z in range(NZ)
    ]


XP, XM, ZP, ZM = ring(1, 0), ring(-1, 0), ring(0, 1), ring(0, -1)
ZGROUPS = [[x * NZ + z for z in range(NZ)] for x in range(NX)]
XGROUPS = [[x * NZ + z for x in range(NX)] for z in range(NZ)]


def pp(value, perm):
    return lax.ppermute(value, "expert", perm)


def add(*terms):
    total = terms[0].astype(f32)
    for term in terms[1:]:
        total = total + term.astype(f32)
    return total.astype(bf16)


def expert_kernel(
    pos, info, *refs
):
    parts, refs = refs[: NZ + 1], refs[NZ + 1 :]
    (a, w_up, w_down, oa, ob, xc_out, sc_out, gp_out, hid_out,
     abuf, bbuf, xc, sc, rc, ko, pt, stage, in_sem, out_sem, save_sem) = refs
    exp_dev, width, _ = w_up.shape
    slots = exp_dev * CAP
    tok, cut_in, cut_out = a.shape[2], a.shape[3], oa.shape[3]
    chosen = info.shape[2] // 2
    zi, xi = pos[0], pos[2]
    base = (pos[1] * slots).astype(f32)

    def turn(i):
        return jnp.where(lax.rem(i, 2) == 1, (i + 1) // 2, lax.rem(NZ - i // 2, NZ))

    def turn(i):
        return jnp.where(lax.rem(i, 2) == 1, (i + 1) // 2, lax.rem(NZ - i // 2, NZ))

    def source(i):
        return lax.rem(zi - turn(i) + NZ, NZ)

    def fetch_a(i, slot):
        return pltpu.make_async_copy(a.at[:, source(i)], abuf.at[slot], in_sem.at[slot, NX])

    def fetch_b(i, slot):
        halves = parts[NZ - 1 :] if i == NZ - 1 else None
        return [
            pltpu.make_async_copy(
                parts[i].at[x] if halves is None else halves[x // 2].at[x % 2],
                bbuf.at[slot, x],
                in_sem.at[slot, x],
            )
            for x in range(NX)
        ]

    def begin(i, slot):
        fetch_a(i, slot).start()
        for step in range(NZ):

            @pl.when(i == step)
            def _():
                for copy in fetch_b(step, slot):
                    copy.start()

    begin(jnp.int32(0), 0)
    row = lax.broadcasted_iota(jnp.int32, (slots, tok), 0).astype(f32)
    lane = lax.broadcasted_iota(jnp.int32, (slots, 128), 1).astype(f32) + 1.0

    def select(z, carry):
        slot = lax.rem(z, 2)

        @pl.when(z + 1 < NZ)
        def _():
            begin(z + 1, 1 - slot)

        fetch_a(z, slot).wait()
        for copy in fetch_b(0, slot):
            copy.wait()
        dz = source(z)
        rest = cut_in - width

        def block(x, inner_carry):
            table = info.at[dz, x]
            which = jnp.zeros((slots, tok), f32)
            gates = jnp.zeros((slots, tok), f32)
            for k in range(chosen):
                eq = (table[k : k + 1, :] - base) == row
                which = jnp.where(eq, k + 1.0, which)
                gates = jnp.where(eq, table[chosen + k : chosen + k + 1, :], gates)
            sel = (which > 0.0).astype(f32)
            pt[z, x] = sel.T.astype(bf16)
            sel = sel.astype(bf16)
            gate = jnp.sum(gates, axis=1, keepdims=True)
            span = pl.ds(pl.multiple_of(x * CAP, CAP), CAP)
            ko[:, z, span, :] = (
                (jnp.sum(which, axis=1, keepdims=True) == lane)
                .astype(bf16)
                .reshape(exp_dev, CAP, 128)
            )
            rows = jnp.dot(sel, abuf[slot, x, :, :width], preferred_element_type=f32)
            xc[:, z, span, :] = rows.astype(bf16).reshape(exp_dev, CAP, width)
            first = jnp.dot(sel, abuf[slot, x, :, width:], preferred_element_type=f32)
            sc[:, z, span, :rest] = (gate * first).astype(bf16).reshape(exp_dev, CAP, rest)
            second = jnp.dot(sel, bbuf[slot, x], preferred_element_type=f32)
            sc[:, z, span, rest:] = (
                (gate * second).astype(bf16).reshape(exp_dev, CAP, width - rest)
            )
            return inner_carry

        lax.fori_loop(0, NX, block, 0)
        return carry

    lax.fori_loop(0, NZ, select, 0)

    def saves(e):
        return (
            pltpu.make_async_copy(xc.at[e], xc_out.at[e], save_sem.at[0, e]),
            pltpu.make_async_copy(sc.at[e], sc_out.at[e], save_sem.at[1, e]),
        )

    rows = NZ * NX * CAP

    def expert(e, carry):
        for copy in saves(e):
            copy.start()
        up = w_up[e]
        pre = jnp.dot(xc[e].reshape(rows, width), up, preferred_element_type=f32)
        act_value, act_slope = gelu_pair(pre)
        hidden = act_value.astype(bf16)
        grad_hidden = jnp.dot(
            sc[e].reshape(rows, width), w_down[e], preferred_element_type=f32
        )
        inner = jnp.sum(hidden.astype(f32) * grad_hidden, axis=1, keepdims=True)
        grad_pre = (grad_hidden * act_slope).astype(bf16)
        gp_out[e] = grad_pre
        hid_out[e] = hidden
        back = lax.dot_general(
            grad_pre, up, (((1,), (1,)), ((), ())), preferred_element_type=f32
        )
        rc[e, :, :, :width] = back.astype(bf16).reshape(NZ, NX * CAP, width)
        marks = ko[e].reshape(rows, 128).astype(f32) * inner
        rc[e, :, :, width:] = marks.astype(bf16).reshape(NZ, NX * CAP, 128)
        return carry

    lax.fori_loop(0, exp_dev, expert, 0)

    def flush(d, slot):
        copies = []
        for x in range(NX):
            copies.append(
                pltpu.make_async_copy(
                    stage.at[slot, x, :, pl.ds(0, cut_out)], oa.at[x, d], out_sem.at[slot, x]
                )
            )
            copies.append(
                pltpu.make_async_copy(
                    stage.at[slot, x, :, pl.ds(cut_out, width + 128 - cut_out)],
                    ob.at[lax.rem(d - zi + NZ, NZ), lax.rem(xi - x + NX, NX)],
                    out_sem.at[slot, NX + x],
                )
            )
        return copies

    def drain(slot):
        for copy in flush(0, slot):
            copy.wait()

    def combine(step, carry):
        slot = lax.rem(step, 2)
        d = source(step)

        @pl.when(step >= 2)
        def _():
            drain(slot)

        for x in range(NX):
            picked = rc[:, step, x * CAP : (x + 1) * CAP, :].reshape(slots, width + 128)
            total = jnp.dot(pt[step, x], picked, preferred_element_type=f32)
            stage[slot, x] = total.astype(bf16)
        for copy in flush(d, slot):
            copy.start()
        return carry

    lax.fori_loop(0, NZ, combine, 0)
    drain(0)
    drain(1)

    def finish(e, carry):
        for copy in saves(e):
            copy.wait()
        return carry

    lax.fori_loop(0, exp_dev, finish, 0)


def expert_call(pos, info, parts, a, w_up, w_down, cut_out):
    exp_dev, width, hid = w_up.shape
    tok, cut_in = a.shape[2], a.shape[3]
    slots, rows = exp_dev * CAP, NZ * NX * CAP
    wide = width + 128
    shape = jax.ShapeDtypeStruct
    vmem = pl.BlockSpec(memory_space=pltpu.VMEM)
    hbm = pl.BlockSpec(memory_space=pl.ANY)
    flops = 2 * exp_dev * rows * width * hid * 3 + 2 * NZ * NX * slots * tok * width * 3
    return pl.pallas_call(
        expert_kernel,
        out_shape=(
            shape((NX, NZ, tok, cut_out), bf16),
            shape((NZ, NX, tok, wide - cut_out), bf16),
            shape((exp_dev, NZ, NX * CAP, width), bf16),
            shape((exp_dev, NZ, NX * CAP, width), bf16),
            shape((exp_dev, rows, hid), bf16),
            shape((exp_dev, rows, hid), bf16),
        ),
        in_specs=[pl.BlockSpec(memory_space=pltpu.SMEM), vmem] + [hbm] * (NZ + 2) + [vmem] * 2,
        out_specs=tuple([hbm] * 4 + [vmem] * 2),
        scratch_shapes=[
            pltpu.VMEM((2, NX, tok, cut_in), bf16),
            pltpu.VMEM((2, NX, tok, 2 * width - cut_in), bf16),
            pltpu.VMEM((exp_dev, NZ, NX * CAP, width), bf16),
            pltpu.VMEM((exp_dev, NZ, NX * CAP, width), bf16),
            pltpu.VMEM((exp_dev, NZ, NX * CAP, wide), bf16),
            pltpu.VMEM((exp_dev, NZ, NX * CAP, 128), bf16),
            pltpu.VMEM((NZ, NX, tok, slots), bf16),
            pltpu.VMEM((2, NX, tok, wide), bf16),
            pltpu.SemaphoreType.DMA((2, NX + 1)),
            pltpu.SemaphoreType.DMA((2, 2 * NX)),
            pltpu.SemaphoreType.DMA((2, exp_dev)),
        ],
        compiler_params=pltpu.CompilerParams(vmem_limit_bytes=62 * 1024 * 1024),
        cost_estimate=pl.CostEstimate(
            flops=flops, bytes_accessed=70 * 1024 * 1024, transcendentals=exp_dev * rows * hid
        ),
        name="experts",
    )(pos, info, *parts, a, w_up, w_down)


def exchange(value, groups):
    return lax.all_to_all(
        value, "expert", split_axis=0, concat_axis=0, axis_index_groups=groups, tiled=True
    )


def copies(value, n):
    return jnp.broadcast_to(value, (n, *value.shape))


def reduce_z(blocks):
    half = blocks.shape[1] // 2
    up, down = pp(blocks[4, :half], ZP), pp(blocks[4, half:], ZM)
    up, down = lax.optimization_barrier((up, down))
    up_sum = jnp.concatenate([add(blocks[3, :half], up), blocks[3, half:]], 0)
    down_sum = jnp.concatenate([blocks[5, :half], add(blocks[5, half:], down)], 0)
    up, down = pp(up_sum, ZP), pp(down_sum, ZM)
    for d in (2, 1):
        up, down = lax.optimization_barrier((up, down))
        up_sum, down_sum = add(blocks[d], up), add(blocks[NZ - d], down)
        up, down = pp(up_sum, ZP), pp(down_sum, ZM)
    return add(blocks[0], up, down)


def wgrad_kernel(rows, grads, out):
    flat = rows[0].reshape(grads.shape[1], rows.shape[3])
    total = lax.dot_general(
        flat, grads[0], (((0,), (0,)), ((), ())), preferred_element_type=f32
    )
    out[0] = total.astype(bf16)


def wgrad_call(rows, grads):
    exp_dev, width, hid = rows.shape[0], rows.shape[3], grads.shape[2]
    count = grads.shape[1]
    return pl.pallas_call(
        wgrad_kernel,
        grid=(exp_dev,),
        out_shape=jax.ShapeDtypeStruct((exp_dev, width, hid), bf16),
        in_specs=[
            pl.BlockSpec((1, *rows.shape[1:]), lambda e: (e, 0, 0, 0)),
            pl.BlockSpec((1, count, hid), lambda e: (e, 0, 0)),
        ],
        out_specs=pl.BlockSpec((1, width, hid), lambda e: (e, 0, 0)),
        compiler_params=pltpu.CompilerParams(vmem_limit_bytes=60 * 1024 * 1024),
        cost_estimate=pl.CostEstimate(
            flops=2 * exp_dev * count * width * hid,
            bytes_accessed=16 * 1024 * 1024,
            transcendentals=0,
        ),
        name="wgrad",
    )(rows, grads)


def final_kernel(za, own, b1, b2, b3, scores, up, down, tok_out, log_out, up_out, down_out):
    width, cut = tok_out.shape[1], za.shape[2]
    chosen = scores.shape[1]
    total = za[0].astype(f32)
    for z in range(1, NZ):
        total = total + za[z].astype(f32)
    tok_out[:, :cut] = total.astype(bf16)
    total = own[0].astype(f32)
    for other in (b1, b2, b3):
        total = total + other[...].astype(f32)
    tok_out[:, cut:] = total[:, : width - cut].astype(bf16)
    inner = total[:, width - cut : width - cut + chosen].astype(bf16).astype(f32)
    log_out[...] = (1.0 - scores[...]) * inner
    up_out[...] = up[...].astype(f32)
    down_out[...] = down[...].astype(f32)


def final_call(za, col, others, scores, up, down, width):
    tok = scores.shape[0]
    full = lambda v: pl.BlockSpec(v.shape, lambda i: (0,) * v.ndim)
    return pl.pallas_call(
        final_kernel,
        grid=(1,),
        out_shape=(
            jax.ShapeDtypeStruct((tok, width), bf16),
            jax.ShapeDtypeStruct(scores.shape, f32),
            jax.ShapeDtypeStruct(up.shape, f32),
            jax.ShapeDtypeStruct(down.shape, f32),
        ),
        in_specs=[full(za), pl.BlockSpec((1, *col.shape[1:]), lambda i: (0, 0, 0))]
        + [full(v) for v in others]
        + [full(scores), full(up), full(down)],
        out_specs=(
            pl.BlockSpec((tok, width), lambda i: (0, 0)),
            full(scores),
            full(up),
            full(down),
        ),
        compiler_params=pltpu.CompilerParams(vmem_limit_bytes=24 * 1024 * 1024),
        name="final",
    )(za, col, *others, scores, up, down)


def gather_b(own):
    half = NX // 2
    parts = [own]
    up = down = own
    for _ in range(1, 4):
        up, down = pp(up, ZP), pp(down, ZM)
        up, down = lax.optimization_barrier((up, down))
        parts += [up, down]
    return [*parts, pp(up[:half], ZP), pp(down[half:], ZM)]


def local(tokens, out_grad, logits, routes, w_up, w_down):
    tok, _ = routes.shape
    exp_dev, width, _ = w_up.shape
    experts = exp_dev * NX * NZ
    me = lax.axis_index("expert")
    scores = jax.nn.sigmoid(logits)
    hit = routes[:, :, None] == jnp.arange(experts, dtype=jnp.int32)
    named = jnp.any(hit, axis=1).astype(bf16)
    before = jnp.tril(jnp.ones((tok, tok), bf16), -1)
    count = jnp.dot(before, named, preferred_element_type=f32)
    rank = jnp.sum(jnp.where(hit, count[:, None, :], 0.0), axis=2)
    info = jnp.concatenate([routes.astype(f32) * CAP + rank, scores], axis=1).T
    groups = 2 * width // 128
    cut = (13 * groups // 24) * 128
    pay = jnp.concatenate([tokens, out_grad], axis=1)
    pa, pb = pay[:, :cut], pay[:, cut:]
    a_all = lax.all_gather(pa, "expert").reshape(NX, NZ, *pa.shape)
    parts = gather_b(exchange(copies(pb, NX), XGROUPS))
    column = exchange(copies(info, NX), XGROUPS)
    infos = exchange(copies(column, NZ), ZGROUPS)
    wide = width + 128
    cut_out = (5 * (wide // 128) // 13) * 128
    pos = jnp.stack([me % NZ, me, me // NZ]).astype(jnp.int32)
    oa, ob, xc, sc, grad_pre, hidden = expert_call(
        pos, infos, parts, a_all, w_up, w_down, cut_out
    )
    col_b = reduce_z(ob)
    ax = exchange(oa, XGROUPS)
    up_grad = wgrad_call(xc, grad_pre)
    down_grad = wgrad_call(sc, hidden)
    za = exchange(add(*[ax[x] for x in range(NX)]), ZGROUPS)
    others = [pp(col_b[dx], perm) for dx, perm in ((1, XM), (2, ring(2, 0)), (3, XP))]
    up, down = (
        lax.psum_scatter(g, "dp", scatter_dimension=1, tiled=True) for g in (up_grad, down_grad)
    )
    return final_call(za, col_b, others, scores, up, down, width)


def solution(mesh):
    rows = P(("dp", "expert"), None)
    weights = P("expert", None, None)
    grads = P("expert", "dp", None)
    return jax.shard_map(
        local,
        mesh=mesh,
        in_specs=(rows, rows, rows, rows, weights, weights),
        out_specs=(rows, rows, grads, grads),
        check_vma=False,
    )
```

```python
import jax
import jax.numpy as jnp
from jax import lax
from jax.experimental import pallas as pl
from jax.experimental.pallas import tpu as pltpu
from jax.sharding import PartitionSpec as P


NX, NZ = 4, 8
CAP = 16
gelu_scale = 0.7978845608028654
gelu_cubic = 0.044715
bf16, f32 = jnp.bfloat16, jnp.float32


def gelu_pair(pre_act):
    inner_arg = gelu_scale * (pre_act + gelu_cubic * pre_act * pre_act * pre_act)
    tanh_val = jnp.tanh(inner_arg)
    act_value = 0.5 * pre_act * (1.0 + tanh_val)
    act_slope = 0.5 * (1.0 + tanh_val) + 0.5 * pre_act * (
        1.0 - tanh_val * tanh_val
    ) * gelu_scale * (1.0 + 3.0 * gelu_cubic * pre_act * pre_act)
    return (act_value, act_slope)


GROUPS = ((0, 1, 7, 2), (6, 3, 5, 4))


def ring(dx, dz):
    return [
        (x * NZ + z, ((x + dx) % NX) * NZ + (z + dz) % NZ) for x in range(NX) for z in range(NZ)
    ]


XP, XM, ZP, ZM = ring(1, 0), ring(-1, 0), ring(0, 1), ring(0, -1)
ZGROUPS = [[x * NZ + z for z in range(NZ)] for x in range(NX)]
XGROUPS = [[x * NZ + z for x in range(NX)] for z in range(NZ)]


def pp(value, perm):
    return lax.ppermute(value, "expert", perm)


def zgather(value):
    return lax.all_gather(value, "expert", axis_index_groups=ZGROUPS, tiled=False)


def add(*terms):
    total = terms[0].astype(f32)
    for term in terms[1:]:
        total = total + term.astype(f32)
    return total.astype(bf16)


def expert_kernel(
    pos, info, *refs
):
    parts, refs = refs[: NX * len(GROUPS)], refs[NX * len(GROUPS) :]
    (b, w_up, w_down, oa, ob, xc_out, sc_out, gp_out, hid_out,
     abuf, bbuf, xc, sc, rc, ko, pt, stage, in_sem, out_sem, save_sem) = refs
    exp_dev, width, _ = w_up.shape
    slots = exp_dev * CAP
    tok = parts[0].shape[1]
    cut_in, cut_out = parts[0].shape[2], oa.shape[3]
    chosen = info.shape[2] // 2
    zi, xi = pos[0], pos[2]
    base = (pos[1] * slots).astype(f32)

    def turn(i):
        return jnp.where(lax.rem(i, 2) == 1, (i + 1) // 2, lax.rem(NZ - i // 2, NZ))

    def x_of(dx):
        return lax.rem(xi - dx + NX, NX)

    def source(i):
        return lax.rem(zi - turn(i) + NZ, NZ)

    def fetch_a(g, j, slot):
        own, plus, minus, far = parts[NX * g : NX * (g + 1)]
        return [
            pltpu.make_async_copy(part.at[j], abuf.at[slot, dx], in_sem.at[slot, dx])
            for dx, part in enumerate((own, plus, far, minus))
        ]

    def fetch_b(i, slot):
        return pltpu.make_async_copy(b.at[source(i)], bbuf.at[slot], in_sem.at[slot, NX])

    def begin(i, slot):
        fetch_b(i, slot).start()
        step = 0
        for g, turns in enumerate(GROUPS):
            for j in range(len(turns)):

                @pl.when(i == step)
                def _():
                    for copy in fetch_a(g, j, slot):
                        copy.start()

                step += 1

    begin(jnp.int32(0), 0)
    row = lax.broadcasted_iota(jnp.int32, (slots, tok), 0).astype(f32)
    lane = lax.broadcasted_iota(jnp.int32, (slots, 128), 1).astype(f32) + 1.0

    def select(z, carry):
        slot = lax.rem(z, 2)

        @pl.when(z + 1 < NZ)
        def _():
            begin(z + 1, 1 - slot)

        fetch_b(z, slot).wait()
        for copy in fetch_a(0, 0, slot):
            copy.wait()
        dz = source(z)
        rest = cut_in - width

        def block(dx, inner_carry):
            table = info.at[dz, x_of(dx)]
            which = jnp.zeros((slots, tok), f32)
            gates = jnp.zeros((slots, tok), f32)
            for k in range(chosen):
                eq = (table[k : k + 1, :] - base) == row
                which = jnp.where(eq, k + 1.0, which)
                gates = jnp.where(eq, table[chosen + k : chosen + k + 1, :], gates)
            sel = (which > 0.0).astype(f32)
            pt[z, dx] = sel.T.astype(bf16)
            sel = sel.astype(bf16)
            gate = jnp.sum(gates, axis=1, keepdims=True)
            span = pl.ds(pl.multiple_of(dx * CAP, CAP), CAP)
            ko[:, z, span, :] = (
                (jnp.sum(which, axis=1, keepdims=True) == lane)
                .astype(bf16)
                .reshape(exp_dev, CAP, 128)
            )
            rows = jnp.dot(sel, abuf[slot, dx, :, :width], preferred_element_type=f32)
            xc[:, z, span, :] = rows.astype(bf16).reshape(exp_dev, CAP, width)
            first = jnp.dot(sel, abuf[slot, dx, :, width:], preferred_element_type=f32)
            sc[:, z, span, :rest] = (gate * first).astype(bf16).reshape(exp_dev, CAP, rest)
            second = jnp.dot(sel, bbuf[slot, x_of(dx)], preferred_element_type=f32)
            sc[:, z, span, rest:] = (
                (gate * second).astype(bf16).reshape(exp_dev, CAP, width - rest)
            )
            return inner_carry

        lax.fori_loop(0, NX, block, 0)
        return carry

    lax.fori_loop(0, NZ, select, 0)

    def saves(e):
        return (
            pltpu.make_async_copy(xc.at[e], xc_out.at[e], save_sem.at[0, e]),
            pltpu.make_async_copy(sc.at[e], sc_out.at[e], save_sem.at[1, e]),
        )

    rows = NZ * NX * CAP

    def expert(e, carry):
        for copy in saves(e):
            copy.start()
        up = w_up[e]
        pre = jnp.dot(xc[e].reshape(rows, width), up, preferred_element_type=f32)
        act_value, act_slope = gelu_pair(pre)
        hidden = act_value.astype(bf16)
        grad_hidden = jnp.dot(
            sc[e].reshape(rows, width), w_down[e], preferred_element_type=f32
        )
        inner = jnp.sum(hidden.astype(f32) * grad_hidden, axis=1, keepdims=True)
        grad_pre = (grad_hidden * act_slope).astype(bf16)
        gp_out[e] = grad_pre
        hid_out[e] = hidden
        back = lax.dot_general(
            grad_pre, up, (((1,), (1,)), ((), ())), preferred_element_type=f32
        )
        rc[e, :, :, :width] = back.astype(bf16).reshape(NZ, NX * CAP, width)
        marks = ko[e].reshape(rows, 128).astype(f32) * inner
        rc[e, :, :, width:] = marks.astype(bf16).reshape(NZ, NX * CAP, 128)
        return carry

    lax.fori_loop(0, exp_dev, expert, 0)

    def flush(d, slot, dx):
        return (
            pltpu.make_async_copy(
                stage.at[slot, dx, :, pl.ds(0, cut_out)],
                oa.at[x_of(dx), d],
                out_sem.at[slot, dx],
            ),
            pltpu.make_async_copy(
                stage.at[slot, dx, :, pl.ds(cut_out, width + 128 - cut_out)],
                ob.at[lax.rem(d - zi + NZ, NZ), dx],
                out_sem.at[slot, NX + dx],
            ),
        )

    def drain(slot):
        def one(dx, carry):
            for copy in flush(0, slot, dx):
                copy.wait()
            return carry

        lax.fori_loop(0, NX, one, 0)

    def combine(step, carry):
        slot = lax.rem(step, 2)
        d = source(step)

        @pl.when(step >= 2)
        def _():
            drain(slot)

        def one(dx, inner_carry):
            span = pl.ds(pl.multiple_of(dx * CAP, CAP), CAP)
            picked = rc[:, step, span, :].reshape(slots, width + 128)
            total = jnp.dot(pt[step, dx], picked, preferred_element_type=f32)
            stage[slot, dx] = total.astype(bf16)
            for copy in flush(d, slot, dx):
                copy.start()
            return inner_carry

        lax.fori_loop(0, NX, one, 0)
        return carry

    lax.fori_loop(0, NZ, combine, 0)
    drain(0)
    drain(1)

    def finish(e, carry):
        for copy in saves(e):
            copy.wait()
        return carry

    lax.fori_loop(0, exp_dev, finish, 0)


def expert_call(pos, info, parts, b, w_up, w_down, cut_out):
    exp_dev, width, hid = w_up.shape
    tok, cut_in = parts[0].shape[1], parts[0].shape[2]
    slots, rows = exp_dev * CAP, NZ * NX * CAP
    wide = width + 128
    shape = jax.ShapeDtypeStruct
    vmem = pl.BlockSpec(memory_space=pltpu.VMEM)
    hbm = pl.BlockSpec(memory_space=pl.ANY)
    flops = 2 * exp_dev * rows * width * hid * 3 + 2 * NZ * NX * slots * tok * width * 3
    return pl.pallas_call(
        expert_kernel,
        out_shape=(
            shape((NX, NZ, tok, cut_out), bf16),
            shape((NZ, NX, tok, wide - cut_out), bf16),
            shape((exp_dev, NZ, NX * CAP, width), bf16),
            shape((exp_dev, NZ, NX * CAP, width), bf16),
            shape((exp_dev, rows, hid), bf16),
            shape((exp_dev, rows, hid), bf16),
        ),
        in_specs=[pl.BlockSpec(memory_space=pltpu.SMEM), vmem] + [hbm] * (NX * len(GROUPS) + 1) + [vmem] * 2,
        out_specs=tuple([hbm] * 4 + [vmem] * 2),
        scratch_shapes=[
            pltpu.VMEM((2, NX, tok, cut_in), bf16),
            pltpu.VMEM((2, NX, tok, 2 * width - cut_in), bf16),
            pltpu.VMEM((exp_dev, NZ, NX * CAP, width), bf16),
            pltpu.VMEM((exp_dev, NZ, NX * CAP, width), bf16),
            pltpu.VMEM((exp_dev, NZ, NX * CAP, wide), bf16),
            pltpu.VMEM((exp_dev, NZ, NX * CAP, 128), bf16),
            pltpu.VMEM((NZ, NX, tok, slots), bf16),
            pltpu.VMEM((2, NX, tok, wide), bf16),
            pltpu.SemaphoreType.DMA((2, NX + 1)),
            pltpu.SemaphoreType.DMA((2, 2 * NX)),
            pltpu.SemaphoreType.DMA((2, exp_dev)),
        ],
        compiler_params=pltpu.CompilerParams(vmem_limit_bytes=62 * 1024 * 1024),
        cost_estimate=pl.CostEstimate(
            flops=flops, bytes_accessed=70 * 1024 * 1024, transcendentals=exp_dev * rows * hid
        ),
        name="experts",
    )(pos, info, *parts, b, w_up, w_down)


def exchange(value, groups):
    return lax.all_to_all(
        value, "expert", split_axis=0, concat_axis=0, axis_index_groups=groups, tiled=True
    )


def copies(value, n):
    return jnp.broadcast_to(value, (n, *value.shape))


def reduce_z(blocks):
    half = blocks.shape[1] // 2
    up, down = pp(blocks[4, :half], ZP), pp(blocks[4, half:], ZM)
    up, down = lax.optimization_barrier((up, down))
    up_sum = jnp.concatenate([add(blocks[3, :half], up), blocks[3, half:]], 0)
    down_sum = jnp.concatenate([blocks[5, :half], add(blocks[5, half:], down)], 0)
    up, down = pp(up_sum, ZP), pp(down_sum, ZM)
    for d in (2, 1):
        up, down = lax.optimization_barrier((up, down))
        up_sum, down_sum = add(blocks[d], up), add(blocks[NZ - d], down)
        up, down = pp(up_sum, ZP), pp(down_sum, ZM)
    return add(blocks[0], up, down)


def wgrad_kernel(rows, grads, out):
    flat = rows[0].reshape(grads.shape[1], rows.shape[3])
    total = lax.dot_general(
        flat, grads[0], (((0,), (0,)), ((), ())), preferred_element_type=f32
    )
    out[0] = total.astype(bf16)


def wgrad_call(rows, grads):
    exp_dev, width, hid = rows.shape[0], rows.shape[3], grads.shape[2]
    count = grads.shape[1]
    return pl.pallas_call(
        wgrad_kernel,
        grid=(exp_dev, 2),
        out_shape=jax.ShapeDtypeStruct((exp_dev, width, hid), bf16),
        in_specs=[
            pl.BlockSpec((1, *rows.shape[1:3], width // 2), lambda e, h: (e, 0, 0, h)),
            pl.BlockSpec((1, count, hid), lambda e, h: (e, 0, 0)),
        ],
        out_specs=pl.BlockSpec((1, width // 2, hid), lambda e, h: (e, h, 0)),
        compiler_params=pltpu.CompilerParams(vmem_limit_bytes=60 * 1024 * 1024),
        cost_estimate=pl.CostEstimate(
            flops=2 * exp_dev * count * width * hid,
            bytes_accessed=16 * 1024 * 1024,
            transcendentals=0,
        ),
        name="wgrad",
    )(rows, grads)


def final_kernel(za, own, b1, b2, b3, scores, tok_out, log_out):
    width, cut = tok_out.shape[1], za.shape[2]
    chosen = scores.shape[1]
    total = za[0].astype(f32)
    for z in range(1, NZ):
        total = total + za[z].astype(f32)
    tok_out[:, :cut] = total.astype(bf16)
    total = own[0].astype(f32)
    for other in (b1, b2, b3):
        total = total + other[...].astype(f32)
    tok_out[:, cut:] = total[:, : width - cut].astype(bf16)
    inner = total[:, width - cut : width - cut + chosen].astype(bf16).astype(f32)
    log_out[...] = (1.0 - scores[...]) * inner


def final_call(za, col, others, scores, width):
    tok = scores.shape[0]
    full = lambda v: pl.BlockSpec(v.shape, lambda i: (0,) * v.ndim)
    return pl.pallas_call(
        final_kernel,
        grid=(1,),
        out_shape=(
            jax.ShapeDtypeStruct((tok, width), bf16),
            jax.ShapeDtypeStruct(scores.shape, f32),
        ),
        in_specs=[full(za), pl.BlockSpec((1, *col.shape[1:]), lambda i: (0, 0, 0))]
        + [full(v) for v in others]
        + [full(scores)],
        out_specs=(
            pl.BlockSpec((tok, width), lambda i: (0, 0)),
            pl.BlockSpec(scores.shape, lambda i: (0, 0)),
        ),
        compiler_params=pltpu.CompilerParams(vmem_limit_bytes=24 * 1024 * 1024),
        name="final",
    )(za, col, *others, scores)


def gather_a(own):
    half = own.shape[0] // 2
    at = {0: own}
    up = down = own
    for d in range(1, 4):
        up, down = pp(up, ZP), pp(down, ZM)
        at[d], at[NZ - d] = up, down
    at[4] = jnp.concatenate([pp(up[:half], ZP), pp(down[half:], ZM)], 0)
    parts = []
    for g, turns in enumerate(GROUPS):
        group = jnp.stack([at[d] for d in turns])
        plus, minus = pp(group, XP), pp(group, XM)
        far = pp(minus, XM) if g else pp(plus, XP)
        parts += [group, plus, minus, far]
    return parts


def local(tokens, out_grad, logits, routes, w_up, w_down):
    tok, _ = routes.shape
    exp_dev, width, _ = w_up.shape
    experts = exp_dev * NX * NZ
    me = lax.axis_index("expert")
    scores = jax.nn.sigmoid(logits)
    hit = routes[:, :, None] == jnp.arange(experts, dtype=jnp.int32)
    named = jnp.any(hit, axis=1).astype(bf16)
    before = jnp.tril(jnp.ones((tok, tok), bf16), -1)
    count = jnp.dot(before, named, preferred_element_type=f32)
    rank = jnp.sum(jnp.where(hit, count[:, None, :], 0.0), axis=2)
    info = jnp.concatenate([routes.astype(f32) * CAP + rank, scores], axis=1).T
    groups = 2 * width // 128
    cut = (15 * groups // 24) * 128
    pay = jnp.concatenate([tokens, out_grad], axis=1)
    pa, pb = pay[:, :cut], pay[:, cut:]
    bx = exchange(copies(pb, NX), XGROUPS)
    bz = zgather(bx)
    column = exchange(copies(info, NX), XGROUPS)
    infos = exchange(copies(column, NZ), ZGROUPS)
    parts = gather_a(pa)
    wide = width + 128
    cut_out = (5 * (wide // 128) // 13) * 128
    pos = jnp.stack([me % NZ, me, me // NZ]).astype(jnp.int32)
    oa, ob, xc, sc, grad_pre, hidden = expert_call(
        pos, infos, parts, bz, w_up, w_down, cut_out
    )
    col_b = reduce_z(ob)
    ax = exchange(oa, XGROUPS)
    up_grad = wgrad_call(xc, grad_pre)
    down_grad = wgrad_call(sc, hidden)
    za = exchange(add(*[ax[x] for x in range(NX)]), ZGROUPS)
    others = [pp(col_b[dx], perm) for dx, perm in ((1, XM), (2, ring(2, 0)), (3, XP))]
    grad_tokens, grad_logits = final_call(za, col_b, others, scores, width)
    grad_up, grad_down = (
        lax.psum_scatter(g, "dp", scatter_dimension=1, tiled=True).astype(f32)
        for g in (up_grad, down_grad)
    )
    return (grad_tokens, grad_logits, grad_up, grad_down)


def solution(mesh):
    rows = P(("dp", "expert"), None)
    weights = P("expert", None, None)
    grads = P("expert", "dp", None)
    return jax.shard_map(
        local,
        mesh=mesh,
        in_specs=(rows, rows, rows, rows, weights, weights),
        out_specs=(rows, rows, grads, grads),
        check_vma=False,
    )
```

```python
import jax
import jax.numpy as jnp
from jax import lax
from jax.experimental import pallas as pl
from jax.experimental.pallas import tpu as pltpu
from jax.sharding import PartitionSpec as P


NX, NZ = 4, 8
CAP = 16
gelu_scale = 0.7978845608028654
gelu_cubic = 0.044715
bf16, f32 = jnp.bfloat16, jnp.float32


def gelu_pair(pre_act):
    inner_arg = gelu_scale * (pre_act + gelu_cubic * pre_act * pre_act * pre_act)
    tanh_val = jnp.tanh(inner_arg)
    act_value = 0.5 * pre_act * (1.0 + tanh_val)
    act_slope = 0.5 * (1.0 + tanh_val) + 0.5 * pre_act * (
        1.0 - tanh_val * tanh_val
    ) * gelu_scale * (1.0 + 3.0 * gelu_cubic * pre_act * pre_act)
    return (act_value, act_slope)


GROUPS = ((0, 1, 7, 2), (6, 3, 5, 4))


def ring(dx, dz):
    return [
        (x * NZ + z, ((x + dx) % NX) * NZ + (z + dz) % NZ) for x in range(NX) for z in range(NZ)
    ]


XP, XM, ZP, ZM = ring(1, 0), ring(-1, 0), ring(0, 1), ring(0, -1)
ZGROUPS = [[x * NZ + z for z in range(NZ)] for x in range(NX)]
XGROUPS = [[x * NZ + z for x in range(NX)] for z in range(NZ)]


def pp(value, perm):
    return lax.ppermute(value, "expert", perm)


def zgather(value):
    return lax.all_gather(value, "expert", axis_index_groups=ZGROUPS, tiled=False)


def add(*terms):
    total = terms[0].astype(f32)
    for term in terms[1:]:
        total = total + term.astype(f32)
    return total.astype(bf16)


def expert_kernel(
    pos, info, *refs
):
    parts, refs = refs[: NX * len(GROUPS)], refs[NX * len(GROUPS) :]
    (b, w_up, w_down, oa, ob, xc_out, sc_out, gp_out, hid_out,
     abuf, bbuf, xc, sc, rc, ko, pt, stage, in_sem, out_sem, save_sem) = refs
    exp_dev, width, _ = w_up.shape
    slots = exp_dev * CAP
    tok = parts[0].shape[1]
    cut_in, cut_out = parts[0].shape[2], oa.shape[3]
    chosen = info.shape[2] // 2
    zi, xi = pos[0], pos[2]
    base = (pos[1] * slots).astype(f32)

    def turn(i):
        return jnp.where(lax.rem(i, 2) == 1, (i + 1) // 2, lax.rem(NZ - i // 2, NZ))

    def x_of(dx):
        return lax.rem(xi - dx + NX, NX)

    def source(i):
        return lax.rem(zi - turn(i) + NZ, NZ)

    def fetch_a(g, j, slot):
        own, plus, minus, far = parts[NX * g : NX * (g + 1)]
        return [
            pltpu.make_async_copy(part.at[j], abuf.at[slot, dx], in_sem.at[slot, dx])
            for dx, part in enumerate((own, plus, far, minus))
        ]

    def fetch_b(i, slot):
        return pltpu.make_async_copy(b.at[source(i)], bbuf.at[slot], in_sem.at[slot, NX])

    def begin(i, slot):
        fetch_b(i, slot).start()
        step = 0
        for g, turns in enumerate(GROUPS):
            for j in range(len(turns)):

                @pl.when(i == step)
                def _():
                    for copy in fetch_a(g, j, slot):
                        copy.start()

                step += 1

    begin(jnp.int32(0), 0)
    row = lax.broadcasted_iota(jnp.int32, (slots, tok), 0).astype(f32)
    lane = lax.broadcasted_iota(jnp.int32, (slots, 128), 1).astype(f32) + 1.0

    def select(z, carry):
        slot = lax.rem(z, 2)

        @pl.when(z + 1 < NZ)
        def _():
            begin(z + 1, 1 - slot)

        fetch_b(z, slot).wait()
        for copy in fetch_a(0, 0, slot):
            copy.wait()
        dz = source(z)
        rest = cut_in - width

        def block(dx, inner_carry):
            table = info.at[dz, x_of(dx)]
            which = jnp.zeros((slots, tok), f32)
            gates = jnp.zeros((slots, tok), f32)
            for k in range(chosen):
                eq = (table[k : k + 1, :] - base) == row
                which = jnp.where(eq, k + 1.0, which)
                gates = jnp.where(eq, table[chosen + k : chosen + k + 1, :], gates)
            sel = (which > 0.0).astype(f32)
            pt[z, dx] = sel.T.astype(bf16)
            sel = sel.astype(bf16)
            gate = jnp.sum(gates, axis=1, keepdims=True)
            span = pl.ds(pl.multiple_of(dx * CAP, CAP), CAP)
            ko[:, z, span, :] = (
                (jnp.sum(which, axis=1, keepdims=True) == lane)
                .astype(bf16)
                .reshape(exp_dev, CAP, 128)
            )
            rows = jnp.dot(sel, abuf[slot, dx, :, :width], preferred_element_type=f32)
            xc[:, z, span, :] = rows.astype(bf16).reshape(exp_dev, CAP, width)
            first = jnp.dot(sel, abuf[slot, dx, :, width:], preferred_element_type=f32)
            sc[:, z, span, :rest] = (gate * first).astype(bf16).reshape(exp_dev, CAP, rest)
            second = jnp.dot(sel, bbuf[slot, x_of(dx)], preferred_element_type=f32)
            sc[:, z, span, rest:] = (
                (gate * second).astype(bf16).reshape(exp_dev, CAP, width - rest)
            )
            return inner_carry

        lax.fori_loop(0, NX, block, 0)
        return carry

    lax.fori_loop(0, NZ, select, 0)

    def saves(e):
        return (
            pltpu.make_async_copy(xc.at[e], xc_out.at[e], save_sem.at[0, e]),
            pltpu.make_async_copy(sc.at[e], sc_out.at[e], save_sem.at[1, e]),
        )

    rows = NZ * NX * CAP

    def expert(e, carry):
        for copy in saves(e):
            copy.start()
        up = w_up[e]
        pre = jnp.dot(xc[e].reshape(rows, width), up, preferred_element_type=f32)
        act_value, act_slope = gelu_pair(pre)
        hidden = act_value.astype(bf16)
        grad_hidden = jnp.dot(
            sc[e].reshape(rows, width), w_down[e], preferred_element_type=f32
        )
        inner = jnp.sum(hidden.astype(f32) * grad_hidden, axis=1, keepdims=True)
        grad_pre = (grad_hidden * act_slope).astype(bf16)
        gp_out[e] = grad_pre
        hid_out[e] = hidden
        back = lax.dot_general(
            grad_pre, up, (((1,), (1,)), ((), ())), preferred_element_type=f32
        )
        rc[e, :, :, :width] = back.astype(bf16).reshape(NZ, NX * CAP, width)
        marks = ko[e].reshape(rows, 128).astype(f32) * inner
        rc[e, :, :, width:] = marks.astype(bf16).reshape(NZ, NX * CAP, 128)
        return carry

    lax.fori_loop(0, exp_dev, expert, 0)

    def flush(d, slot, dx):
        return (
            pltpu.make_async_copy(
                stage.at[slot, dx, :, pl.ds(0, cut_out)],
                oa.at[x_of(dx), d],
                out_sem.at[slot, dx],
            ),
            pltpu.make_async_copy(
                stage.at[slot, dx, :, pl.ds(cut_out, width + 128 - cut_out)],
                ob.at[lax.rem(d - zi + NZ, NZ), dx],
                out_sem.at[slot, NX + dx],
            ),
        )

    def drain(slot):
        def one(dx, carry):
            for copy in flush(0, slot, dx):
                copy.wait()
            return carry

        lax.fori_loop(0, NX, one, 0)

    def combine(step, carry):
        slot = lax.rem(step, 2)
        d = source(step)

        @pl.when(step >= 2)
        def _():
            drain(slot)

        def one(dx, inner_carry):
            span = pl.ds(pl.multiple_of(dx * CAP, CAP), CAP)
            picked = rc[:, step, span, :].reshape(slots, width + 128)
            total = jnp.dot(pt[step, dx], picked, preferred_element_type=f32)
            stage[slot, dx] = total.astype(bf16)
            for copy in flush(d, slot, dx):
                copy.start()
            return inner_carry

        lax.fori_loop(0, NX, one, 0)
        return carry

    lax.fori_loop(0, NZ, combine, 0)
    drain(0)
    drain(1)

    def finish(e, carry):
        for copy in saves(e):
            copy.wait()
        return carry

    lax.fori_loop(0, exp_dev, finish, 0)


def expert_call(pos, info, parts, b, w_up, w_down, cut_out):
    exp_dev, width, hid = w_up.shape
    tok, cut_in = parts[0].shape[1], parts[0].shape[2]
    slots, rows = exp_dev * CAP, NZ * NX * CAP
    wide = width + 128
    shape = jax.ShapeDtypeStruct
    vmem = pl.BlockSpec(memory_space=pltpu.VMEM)
    hbm = pl.BlockSpec(memory_space=pl.ANY)
    flops = 2 * exp_dev * rows * width * hid * 3 + 2 * NZ * NX * slots * tok * width * 3
    return pl.pallas_call(
        expert_kernel,
        out_shape=(
            shape((NX, NZ, tok, cut_out), bf16),
            shape((NZ, NX, tok, wide - cut_out), bf16),
            shape((exp_dev, NZ, NX * CAP, width), bf16),
            shape((exp_dev, NZ, NX * CAP, width), bf16),
            shape((exp_dev, rows, hid), bf16),
            shape((exp_dev, rows, hid), bf16),
        ),
        in_specs=[pl.BlockSpec(memory_space=pltpu.SMEM), vmem] + [hbm] * (NX * len(GROUPS) + 1) + [vmem] * 2,
        out_specs=tuple([hbm] * 4 + [vmem] * 2),
        scratch_shapes=[
            pltpu.VMEM((2, NX, tok, cut_in), bf16),
            pltpu.VMEM((2, NX, tok, 2 * width - cut_in), bf16),
            pltpu.VMEM((exp_dev, NZ, NX * CAP, width), bf16),
            pltpu.VMEM((exp_dev, NZ, NX * CAP, width), bf16),
            pltpu.VMEM((exp_dev, NZ, NX * CAP, wide), bf16),
            pltpu.VMEM((exp_dev, NZ, NX * CAP, 128), bf16),
            pltpu.VMEM((NZ, NX, tok, slots), bf16),
            pltpu.VMEM((2, NX, tok, wide), bf16),
            pltpu.SemaphoreType.DMA((2, NX + 1)),
            pltpu.SemaphoreType.DMA((2, 2 * NX)),
            pltpu.SemaphoreType.DMA((2, exp_dev)),
        ],
        compiler_params=pltpu.CompilerParams(vmem_limit_bytes=62 * 1024 * 1024),
        cost_estimate=pl.CostEstimate(
            flops=flops, bytes_accessed=70 * 1024 * 1024, transcendentals=exp_dev * rows * hid
        ),
        name="experts",
    )(pos, info, *parts, b, w_up, w_down)


def exchange(value, groups):
    return lax.all_to_all(
        value, "expert", split_axis=0, concat_axis=0, axis_index_groups=groups, tiled=True
    )


def copies(value, n):
    return jnp.broadcast_to(value, (n, *value.shape))


def reduce_z(blocks):
    half = blocks.shape[1] // 2
    up, down = pp(blocks[4, :half], ZP), pp(blocks[4, half:], ZM)
    up, down = lax.optimization_barrier((up, down))
    up_sum = jnp.concatenate([add(blocks[3, :half], up), blocks[3, half:]], 0)
    down_sum = jnp.concatenate([blocks[5, :half], add(blocks[5, half:], down)], 0)
    up, down = pp(up_sum, ZP), pp(down_sum, ZM)
    for d in (2, 1):
        up, down = lax.optimization_barrier((up, down))
        up_sum, down_sum = add(blocks[d], up), add(blocks[NZ - d], down)
        up, down = pp(up_sum, ZP), pp(down_sum, ZM)
    return add(blocks[0], up, down)


def wgrad_kernel(rows, grads, out):
    flat = rows[0].reshape(grads.shape[1], rows.shape[3])
    total = lax.dot_general(
        flat, grads[0], (((0,), (0,)), ((), ())), preferred_element_type=f32
    )
    out[0] = total.astype(bf16)


def wgrad_call(rows, grads):
    exp_dev, width, hid = rows.shape[0], rows.shape[3], grads.shape[2]
    count = grads.shape[1]
    return pl.pallas_call(
        wgrad_kernel,
        grid=(exp_dev, 2),
        out_shape=jax.ShapeDtypeStruct((exp_dev, width, hid), bf16),
        in_specs=[
            pl.BlockSpec((1, *rows.shape[1:3], width // 2), lambda e, h: (e, 0, 0, h)),
            pl.BlockSpec((1, count, hid), lambda e, h: (e, 0, 0)),
        ],
        out_specs=pl.BlockSpec((1, width // 2, hid), lambda e, h: (e, h, 0)),
        compiler_params=pltpu.CompilerParams(vmem_limit_bytes=60 * 1024 * 1024),
        cost_estimate=pl.CostEstimate(
            flops=2 * exp_dev * count * width * hid,
            bytes_accessed=16 * 1024 * 1024,
            transcendentals=0,
        ),
        name="wgrad",
    )(rows, grads)


def final_kernel(za, own, b1, b2, b3, scores, up, tok_out, log_out, up_out):
    width, cut = tok_out.shape[1], za.shape[2]
    chosen = scores.shape[1]
    total = za[0].astype(f32)
    for z in range(1, NZ):
        total = total + za[z].astype(f32)
    tok_out[:, :cut] = total.astype(bf16)
    total = own[0].astype(f32)
    for other in (b1, b2, b3):
        total = total + other[...].astype(f32)
    tok_out[:, cut:] = total[:, : width - cut].astype(bf16)
    inner = total[:, width - cut : width - cut + chosen].astype(bf16).astype(f32)
    log_out[...] = (1.0 - scores[...]) * inner
    up_out[...] = up[...].astype(f32)


def final_call(za, col, others, scores, up, width):
    tok = scores.shape[0]
    full = lambda v: pl.BlockSpec(v.shape, lambda i: (0,) * v.ndim)
    return pl.pallas_call(
        final_kernel,
        grid=(1,),
        out_shape=(
            jax.ShapeDtypeStruct((tok, width), bf16),
            jax.ShapeDtypeStruct(scores.shape, f32),
            jax.ShapeDtypeStruct(up.shape, f32),
        ),
        in_specs=[full(za), pl.BlockSpec((1, *col.shape[1:]), lambda i: (0, 0, 0))]
        + [full(v) for v in others]
        + [full(scores), full(up)],
        out_specs=(
            pl.BlockSpec((tok, width), lambda i: (0, 0)),
            full(scores),
            full(up),
        ),
        compiler_params=pltpu.CompilerParams(vmem_limit_bytes=24 * 1024 * 1024),
        name="final",
    )(za, col, *others, scores, up)


def gather_a(own):
    half = own.shape[0] // 2
    at = {0: own}
    up = down = own
    for d in range(1, 4):
        up, down = pp(up, ZP), pp(down, ZM)
        at[d], at[NZ - d] = up, down
    at[4] = jnp.concatenate([pp(up[:half], ZP), pp(down[half:], ZM)], 0)
    parts = []
    for g, turns in enumerate(GROUPS):
        group = jnp.stack([at[d] for d in turns])
        plus, minus = pp(group, XP), pp(group, XM)
        far = pp(minus, XM) if g else pp(plus, XP)
        parts += [group, plus, minus, far]
    return parts


def local(tokens, out_grad, logits, routes, w_up, w_down):
    tok, _ = routes.shape
    exp_dev, width, _ = w_up.shape
    experts = exp_dev * NX * NZ
    me = lax.axis_index("expert")
    scores = jax.nn.sigmoid(logits)
    hit = routes[:, :, None] == jnp.arange(experts, dtype=jnp.int32)
    named = jnp.any(hit, axis=1).astype(bf16)
    before = jnp.tril(jnp.ones((tok, tok), bf16), -1)
    count = jnp.dot(before, named, preferred_element_type=f32)
    rank = jnp.sum(jnp.where(hit, count[:, None, :], 0.0), axis=2)
    info = jnp.concatenate([routes.astype(f32) * CAP + rank, scores], axis=1).T
    groups = 2 * width // 128
    cut = (15 * groups // 24) * 128
    pay = jnp.concatenate([tokens, out_grad], axis=1)
    pa, pb = pay[:, :cut], pay[:, cut:]
    bx = exchange(copies(pb, NX), XGROUPS)
    bz = zgather(bx)
    column = exchange(copies(info, NX), XGROUPS)
    infos = exchange(copies(column, NZ), ZGROUPS)
    parts = gather_a(pa)
    wide = width + 128
    cut_out = (5 * (wide // 128) // 13) * 128
    pos = jnp.stack([me % NZ, me, me // NZ]).astype(jnp.int32)
    oa, ob, xc, sc, grad_pre, hidden = expert_call(
        pos, infos, parts, bz, w_up, w_down, cut_out
    )
    col_b = reduce_z(ob)
    ax = exchange(oa, XGROUPS)
    up_grad = wgrad_call(xc, grad_pre)
    down_grad = wgrad_call(sc, hidden)
    za = exchange(add(*[ax[x] for x in range(NX)]), ZGROUPS)
    others = [pp(col_b[dx], perm) for dx, perm in ((1, XM), (2, ring(2, 0)), (3, XP))]
    up, down = (
        lax.psum_scatter(g, "dp", scatter_dimension=1, tiled=True) for g in (up_grad, down_grad)
    )
    grad_tokens, grad_logits, grad_up = final_call(za, col_b, others, scores, up, width)
    return (grad_tokens, grad_logits, grad_up, down.astype(f32))


def solution(mesh):
    rows = P(("dp", "expert"), None)
    weights = P("expert", None, None)
    grads = P("expert", "dp", None)
    return jax.shard_map(
        local,
        mesh=mesh,
        in_specs=(rows, rows, rows, rows, weights, weights),
        out_specs=(rows, rows, grads, grads),
        check_vma=False,
    )
```
